32 devices in a mesh: tm: 4 (over z), space: 8 (over y, x, core).
Axes of the slice: x: 2, y: 2, z: 4, core: 2. Of those that a mesh axis runs over, the one named last changes fastest.
Arguments:
- right_side: float32 [64, 2048, 128], P('space', 'tm'), may hold values from -3 to 3
- blocks: float32 [64, 7, 128, 128], P('space'), may hold values from -0.1875 to 0.1875
- neighbors: int32 [64, 7], P('space'), may hold values from 0 to 63, as said below
- shift_rates: float32 [4], replicated, may hold values from 5 to 8
Outputs:
- correction: float32 [64, 2048, 128], P('space', 'tm')
The draws below stay inside these ranges and needn't reach their ends.
Inputs may be any that keep to these rules, and one draw needn't show every extreme that they name: The elements form planes of 8 consecutive elements. neighbors[e, 0] = e. With q the plane of e, column 1 names an element of plane q - 1 and column 2 one of plane q + 1, cyclically over the planes; within a plane, each of these two columns names every element of the neighbouring plane exactly once. Columns 3 to 6 name elements of plane q.
All inputs are finite; a program needn't handle non-finite values.
Results may differ from the reference program's by a relative error of at most 0.0003.
Values sent between devices are 32-bit elements; how exact they have to be, the bound alone decides.
A program may use at most 128 MiB of HBM per device.

```python
import math
import jax
import jax.numpy as jnp
from jax import lax

P_SIZE = 128
L = 2048
E_DEV = 8
SWEEPS = 4
ELEMS = 64


def permuted_row(subkey):
    return jax.random.permutation(subkey, E_DEV)


def draw_neighbors(key, part):
    plane_count = ELEMS // E_DEV
    element = jnp.arange(ELEMS, dtype=jnp.int32)
    plane_of = element // E_DEV
    subkeys = jax.random.split(jax.random.fold_in(key, 11), 2 * plane_count)
    shuffles = jax.vmap(permuted_row)(subkeys).astype(jnp.int32)
    before = shuffles[:plane_count].reshape(-1)
    after = shuffles[plane_count:].reshape(-1)
    prev_plane = (plane_of - 1) % plane_count
    next_plane = (plane_of + 1) % plane_count
    column_before = prev_plane * E_DEV + before
    column_after = next_plane * E_DEV + after
    inside = jax.random.randint(jax.random.fold_in(key, 12), (ELEMS, 4), 0, E_DEV, dtype=jnp.int32)
    inside = inside + (plane_of * E_DEV)[:, None]
    return jnp.concatenate([element[:, None], column_before[:, None], column_after[:, None], inside], 1)


def levels(rng, shape, shards, smallest, top_value):
    def one(position, parts):
        draws = jax.random.uniform(jax.random.fold_in(jax.random.fold_in(rng, 6), position), (parts,), jnp.float32, smallest / len(shards), top_value / len(shards))
        return jnp.repeat(jnp.exp(draws), shape[position] // parts).reshape((-1,) + (1,) * (len(shape) - position - 1))

    factor_of = one(*shards[0])
    for cut in shards[1:]:
        factor_of = factor_of * one(*cut)
    return factor_of


def gaussian(stream_key, shape, scale, limit, cuts=(), kind=jnp.bfloat16):
    entries = scale * jax.random.normal(stream_key, shape, jnp.float32)
    if cuts:
        entries = entries * levels(stream_key, shape, cuts, -0.22, 0.18)
    return jnp.clip(entries, -limit, limit).astype(kind)


def setup_inputs(seed: int = 0) -> dict:
    key_list = jax.random.split(jax.random.key(seed), 5)
    return {
        "right_side": gaussian(key_list[0], (ELEMS, L, P_SIZE), 0.5, 3.0, ((0, 8), (1, 4)), jnp.float32),
        "blocks": gaussian(key_list[1], (ELEMS, 7, P_SIZE, P_SIZE), (7 * P_SIZE) ** -0.5, 0.1875, ((0, 8),), jnp.float32),
        "neighbors": draw_neighbors(jax.random.fold_in(key_list[4], 71), 0),
        "shift_rates": jnp.clip(jax.random.uniform(key_list[3], (SWEEPS,), jnp.float32, 5.0, 8.0), 5.0, 8.0),
    }


WRAP_WEIGHT = 0.01
DIAG_WEIGHT = 6.0
BLOCK_WEIGHT = 3.0
STEP_SCALE = 0.1
EXACT_DOTS = lax.Precision.HIGHEST


def apply_operator(values, blocks, neighbors):
    def add_slot(slot_index, running):
        taken = jnp.take(values, neighbors[:, slot_index], axis=0)
        matrix = lax.dynamic_index_in_dim(blocks, slot_index, 1, keepdims=False)
        return running + jnp.einsum("eij,elj->eli", matrix, taken, precision=EXACT_DOTS)

    summed = lax.fori_loop(0, 7, add_slot, jnp.zeros_like(values))
    return STEP_SCALE * (DIAG_WEIGHT * values + BLOCK_WEIGHT * summed)


def reference(right_side, blocks, neighbors, shift_rates):
    moments = jnp.arange(L).astype(jnp.float32)
    growth = jnp.exp(moments * (math.log(WRAP_WEIGHT) / L))
    scaled = right_side * growth[None, :, None]
    spectrum = jnp.fft.fft(scaled, axis=1)
    spec_real = jnp.real(spectrum).astype(jnp.float32)
    spec_imag = jnp.imag(spectrum).astype(jnp.float32)
    decay_root = math.exp(math.log(WRAP_WEIGHT) / L)
    phases = moments * (2.0 * math.pi / L)
    shift_real = (1.0 - decay_root * jnp.cos(phases))[None, :, None]
    shift_imag = (decay_root * jnp.sin(phases))[None, :, None]
    iter_real = jnp.zeros_like(spec_real)
    iter_imag = jnp.zeros_like(spec_real)
    for sweep_index in range(SWEEPS):
        if sweep_index == 0:
            res_real = spec_real
            res_imag = spec_imag
        else:
            res_real = spec_real - (shift_real * iter_real - shift_imag * iter_imag) - apply_operator(iter_real, blocks, neighbors)
            res_imag = spec_imag - (shift_real * iter_imag + shift_imag * iter_real) - apply_operator(iter_imag, blocks, neighbors)
        den_real = shift_real + STEP_SCALE * shift_rates[sweep_index]
        den_imag = shift_imag
        magnitude = den_real * den_real + den_imag * den_imag
        inv_real = den_real / magnitude
        inv_imag = -den_imag / magnitude
        iter_real, iter_imag = (iter_real + inv_real * res_real - inv_imag * res_imag,
                                iter_imag + inv_real * res_imag + inv_imag * res_real)
    returned = jnp.fft.ifft(lax.complex(iter_real, iter_imag), axis=1)
    return jnp.real(returned) / growth[None, :, None]
```

```python
import functools

import jax
import jax.numpy as jnp
from jax import lax
from jax.experimental import pallas as pl
from jax.experimental.pallas import tpu as pltpu
from jax.sharding import PartitionSpec as P

SWEEPS = 4
SLOTS = 7
PIECES = (2, 2, 2, 1, 1)
CHUNKS = len(PIECES)
ROWS = 8
WRAP_WEIGHT = 0.01
DIAG_WEIGHT = 6.0
BLOCK_WEIGHT = 3.0
STEP_SCALE = 0.1
MESH = pl.DeviceIdType.MESH


def split(value):
    hi = value.astype(jnp.bfloat16)
    lo = (value - hi.astype(jnp.float32)).astype(jnp.bfloat16)
    return hi, lo


def windows(half):
    unit = half // sum(PIECES)
    return [(unit * sum(PIECES[:c]), unit * PIECES[c]) for c in range(CHUNKS)]


def shares(tm_size, plane):
    counts = [plane // tm_size + (t < plane % tm_size) for t in range(tm_size)]
    for inner, outer in ((1, 0), (tm_size - 2, tm_size - 1)):
        if tm_size >= 4 and counts[inner] > 1:
            counts[inner] -= 1
            counts[outer] += 1
    owner = [t for t in range(tm_size) for _ in range(counts[t])]
    place = [sum(o == owner[e] for o in owner[:e]) for e in range(plane)]
    orders = [
        sorted(range(plane), key=lambda e: (place[e] + abs(owner[e] - t), abs(owner[e] - t)))
        for t in range(tm_size)
    ]
    return owner, orders


def kernel(
    tm_size, sp_size, x_ref, blocks_ref, near_ref, shift_ref,
    series_ref, table_ref, start_ref, *scratch
):
    plane, steps, nodes = x_ref.shape
    half = steps // 2
    spans = windows(half)
    moves = SWEEPS - 1
    groups = sp_size // 4
    segments = 2 * tm_size
    first_z = scratch[:CHUNKS]
    halos = scratch[CHUNKS : CHUNKS + 2 * moves * CHUNKS]
    (z1, z2, z3, series, held, weights, table, gathered, own, nearv, nears,
     w_recv, w_out, w_mate, w_fwd, d_recv, d_mate, d_out, n_recv, n_send, n_load,
     h_send, h_recv, r_send, r_recv, e_send, e_recv, t_store) = scratch[
        CHUNKS + 2 * moves * CHUNKS :
    ]
    zs = [None, z1, z2, z3]
    owner, orders = shares(tm_size, plane)
    tm = lax.axis_index("tm")
    sp = lax.axis_index("space")
    group = sp // 4
    chip = (sp // 2) % 2
    core = sp % 2
    far_side = (chip + core) % 2
    far = far_side == 1
    near = far_side == 0
    mate = group * 4 + chip * 2 + (1 - core)
    here_near = group * 4 + chip * 2 + chip
    there_far = group * 4 + (1 - chip) * 2 + chip
    across = ((group + groups + 2 * core - 1) % groups) * 4 + chip * 2 + (1 - core)

    def remote(src, dst, send, recv, **device):
        return pltpu.make_async_remote_copy(
            src_ref=src, dst_ref=dst, send_sem=send, recv_sem=recv,
            device_id=device, device_id_type=MESH,
        )

    def arrived(dst, recv):
        remote(dst, dst, n_send.at[0], recv, space=mate).wait_recv()

    barrier = pltpu.get_barrier_semaphore()
    greeted = 0
    for r in range(tm_size):
        for d in range(4):
            if r == 0 and d == 0:
                continue
            pl.semaphore_signal(
                barrier, inc=1, device_id_type=MESH,
                device_id={"tm": (tm + r) % tm_size, "space": group * 4 + (sp + d) % 4},
            )
            greeted += 1
    if groups > 1:
        pl.semaphore_signal(barrier, inc=1, device_id={"space": across}, device_id_type=MESH)
        greeted += 1

    def ranked(i):
        value = jnp.int32(orders[0][i])
        for t in range(1, tm_size):
            value = jnp.where(tm == t, jnp.int32(orders[t][i]), value)
        return value

    def owner_of(e):
        value = jnp.int32(owner[0])
        for k in range(1, plane):
            value = jnp.where(e == k, jnp.int32(owner[k]), value)
        return value

    def own_load(e):
        return pltpu.make_async_copy(blocks_ref.at[e], held.at[0, e], w_recv.at[0, e])

    def own_data(k):
        first, width = spans[k]
        return pltpu.make_async_copy(
            x_ref.at[:, pl.ds(chip * half + first, width), :], first_z[k].at[0], d_recv.at[k, 0]
        )

    def mate_data(k):
        first, width = spans[k]
        return remote(
            x_ref.at[:, pl.ds(chip * half + first, width), :], first_z[k].at[1],
            d_mate.at[k], d_recv.at[k, 1], space=mate,
        )

    def out_data(k):
        first, width = spans[k]
        return remote(
            x_ref.at[:, pl.ds((1 - chip) * half + first, width), :], first_z[k].at[far_side],
            d_out.at[k], d_recv.at[k, far_side], space=there_far,
        )

    def out_blocks(lp, e):
        return remote(
            blocks_ref.at[e] if lp == 0 else held.at[1, e], held.at[lp, e],
            w_out.at[lp, e], w_recv.at[lp, e], space=there_far,
        )

    def mate_blocks(e):
        return remote(
            blocks_ref.at[e], held.at[1, e], w_mate.at[e], w_recv.at[1, e], space=mate
        )

    def out_near():
        return remote(
            near_ref, nearv.at[far_side], n_send.at[0], n_recv.at[far_side], space=there_far
        )

    def mate_near():
        return remote(near_ref, nearv.at[1], n_send.at[1], n_recv.at[1], space=mate)

    def forward(lp, e, up):
        return remote(
            held.at[lp, e], held.at[lp, e], w_fwd.at[lp, e, up], w_recv.at[lp, e],
            tm=tm + 1 if up else tm - 1,
        )

    def forwards(lp, e, act):
        source = owner_of(e)

        @pl.when((tm <= source) & (tm > 0))
        def _():
            act(forward(lp, e, 0))

        @pl.when((tm >= source) & (tm < tm_size - 1))
        def _():
            act(forward(lp, e, 1))

    def halo(j, k, d):
        return halos[(j * CHUNKS + k) * 2 + d]

    def part(j, k, lp):
        if j == 0:
            return first_z[k].at[lp]
        return zs[j].at[lp, :, pl.ds(*spans[k]), :]

    def transfer(j, k, d):
        return remote(
            part(j, k, d), halo(j, k, d), h_send.at[j, k, d], h_recv.at[j, k, d],
            space=across if d == 0 else mate,
        )

    @pl.when(near)
    def _():
        for e in range(plane):
            own_load(e).start()
        for k in range(CHUNKS):
            own_data(k).start()
        pltpu.make_async_copy(near_ref, nearv.at[0], n_recv.at[0]).start()

    pl.semaphore_wait(barrier, greeted)

    @pl.when(near)
    def _():
        out_near().start()
        for e in range(plane):
            @pl.when(tm == owner[e])
            def _():
                out_blocks(0, e).start()

    @pl.when(far)
    def _():
        out_near().start()
        mate_near().start()
        for k in range(CHUNKS):
            mate_data(k).start()
        for i in range(plane):
            mate_blocks(ranked(i)).start()

    sigmas = [STEP_SCALE * shift_ref[i] for i in range(SWEEPS)]
    rates = [1.0 / (1.0 + jnp.full((ROWS, nodes), sigma, jnp.float32)) for sigma in sigmas]

    def cascade(inputs, states):
        states = list(states)
        above = None
        for i in reversed(range(SWEEPS)):
            total = states[i] if inputs is None else inputs[i] + states[i]
            if above is not None:
                total = total + above
            states[i] = above = rates[i] * total
        return states

    row = lax.broadcasted_iota(jnp.int32, (ROWS, nodes), 0)
    unit = [(row == i).astype(jnp.float32) for i in range(SWEEPS)]

    def respond(g, states):
        kept = []
        for _ in range(ROWS):
            states = cascade(None, states)
            kept.append(states[0])
        flat = jnp.swapaxes(jnp.stack(kept), 0, 1)
        base = pl.multiple_of(g * ROWS, ROWS)
        for j in range(SWEEPS):
            table[j, pl.ds(base, ROWS), :] = flat[j]
        return tuple(states)

    over = lax.fori_loop(0, half // ROWS, respond, tuple(unit))
    save_table = pltpu.make_async_copy(table, table_ref, t_store.at[0])
    save_table.start()
    carry_of = [[over[i][j : j + 1, :] for j in range(SWEEPS)] for i in range(SWEEPS)]

    def advance(vectors):
        result = []
        for i in range(SWEEPS):
            total = carry_of[i][i] * vectors[i]
            for j in range(i + 1, SWEEPS):
                total = total + carry_of[i][j] * vectors[j]
            result.append(total)
        return result

    around = list(over)
    for _ in range(segments - 1):
        around = advance(around)

    def prepare(lp, e):
        outer_slot = 1 + (core if lp == 0 else 1 - core)
        for b in range(SLOTS):
            s = outer_slot if b == 1 else 3 - outer_slot if b == 2 else b
            hi, lo = split((-STEP_SCALE * BLOCK_WEIGHT) * held[lp, e, s].T)
            weights[lp, e, b * nodes : (b + 1) * nodes, :nodes] = hi
            weights[lp, e, b * nodes : (b + 1) * nodes, nodes:] = lo

    def prepare_all(lp):
        def one(e, _):
            prepare(lp, e)
            return 0

        lax.fori_loop(0, plane, one, 0)

    @pl.when(near)
    def _():
        for i in range(plane):
            e = ranked(i)
            arrived(held.at[1, e], w_recv.at[1, e])

            @pl.when(tm == owner_of(e))
            def _():
                out_blocks(1, e).start()

        for k in range(CHUNKS):
            out_data(k).start()
        for k in range(CHUNKS):
            for lp in range(2):
                arrived(first_z[k].at[lp], d_recv.at[k, lp])
                transfer(0, k, lp).start()
        for e in range(plane):
            own_load(e).wait()
        prepare_all(0)
        prepare_all(1)

    def receive(lp, i):
        e = ranked(i)
        arrived(held.at[lp, e], w_recv.at[lp, e])
        forwards(lp, e, lambda copy: copy.start())
        return e

    @pl.when(far)
    def _():
        for i in range(plane):
            prepare(0, receive(0, i))

    for lp in range(2):
        arrived(nearv.at[lp], n_recv.at[lp])
    load_near = pltpu.make_async_copy(nearv, nears, n_load.at[0])
    load_near.start()
    load_near.wait()

    def apply(j, k, lp):
        first, width = spans[k]
        window = pl.ds(first, width)
        diag = sigmas[j] - STEP_SCALE * DIAG_WEIGHT
        outer_slot = 1 + (core if lp == 0 else 1 - core)

        def source(q, index):
            return first_z[k][q, index] if j == 0 else zs[j][q, index, window, :]

        def one(e, _):
            def near_of(s):
                return lax.rem(nears[lp, e, s], plane)

            here = source(lp, e)
            parts = [
                here,
                halo(j, k, lp)[near_of(outer_slot)],
                source(1 - lp, near_of(3 - outer_slot)),
            ] + [source(lp, near_of(s)) for s in range(3, SLOTS)]
            pairs = [split(p) for p in parts]
            hi = jnp.concatenate([p[0] for p in pairs], axis=1)
            lo = jnp.concatenate([p[1] for p in pairs], axis=1)
            both = jnp.dot(hi, weights[lp, e], preferred_element_type=jnp.float32)
            both = both + jnp.dot(lo, weights[lp, e], preferred_element_type=jnp.float32)
            zs[j + 1][lp, e, window, :] = diag * here + both[:, :nodes] + both[:, nodes:]
            return 0

        lax.fori_loop(0, plane, one, 0)

    due = [(plane * (k + 1)) // CHUNKS for k in range(CHUNKS)]
    shared = max(sum(o == t for o in owner) for t in range(tm_size))
    for k in range(CHUNKS):

        @pl.when(far)
        def _():
            for i in range(due[k - 1] if k else 0, due[k]):
                e = receive(1, i)
                if i == min(shared, due[0]) - 1:
                    for c in range(CHUNKS):
                        out_data(c).start()
                prepare(1, e)
            for lp in range(2):
                arrived(first_z[k].at[lp], d_recv.at[k, lp])
                transfer(0, k, lp).start()

        transfer(0, k, 0).wait_recv()
        apply(0, k, 0)
        transfer(1, k, 0).start()

    for k in range(CHUNKS):
        transfer(0, k, 1).wait_recv()
        apply(0, k, 1)
        transfer(1, k, 1).start()

    for k in range(CHUNKS):
        for lp in range(2):
            transfer(1, k, lp).wait_recv()
            apply(1, k, lp)
            transfer(2, k, lp).start()

    def back_target(lp):
        return group * 4 + 2 * core + (core + lp) % 2

    def give_back(k, lp):
        first, width = spans[k]
        return remote(
            series.at[lp, :, pl.ds(first, width), :],
            series_ref.at[:, pl.ds(chip * half + first, width), :],
            r_send.at[k, lp], r_recv.at[k, chip], space=back_target(lp),
        )

    def keep_back(k):
        first, width = spans[k]
        return pltpu.make_async_copy(
            series.at[0, :, pl.ds(first, width), :],
            series_ref.at[:, pl.ds(chip * half + first, width), :],
            r_recv.at[k, chip],
        )

    states = tuple(jnp.zeros((ROWS, nodes), jnp.float32) for _ in range(2 * SWEEPS))
    for k in range(CHUNKS):
        first, width = spans[k]
        for lp in range(2):
            transfer(2, k, lp).wait_recv()
            apply(2, k, lp)

        def scan(g, states):
            states = list(states)
            base = pl.multiple_of(first + g * ROWS, ROWS)
            inner = pl.multiple_of(g * ROWS, ROWS)
            for lp in range(2):
                mine = states[lp * SWEEPS : (lp + 1) * SWEEPS]
                here = [jnp.swapaxes(first_z[k][lp, :, pl.ds(inner, ROWS), :], 0, 1)] + [
                    jnp.swapaxes(z[lp, :, pl.ds(base, ROWS), :], 0, 1) for z in zs[1:]
                ]
                kept = []
                for t in range(ROWS):
                    mine = cascade([h[t] for h in here], mine)
                    kept.append(mine[0])
                series[lp, :, pl.ds(base, ROWS), :] = jnp.swapaxes(jnp.stack(kept), 0, 1)
                states[lp * SWEEPS : (lp + 1) * SWEEPS] = mine
            return tuple(states)

        states = lax.fori_loop(0, width // ROWS, scan, states)
        give_back(k, 1).start()

        @pl.when(far)
        def _():
            give_back(k, 0).start()

        @pl.when(near)
        def _():
            keep_back(k).start()

    for lp in range(2):
        for i in range(SWEEPS):
            own[lp, i] = states[lp * SWEEPS + i]
    segment = 2 * tm + chip

    def give_end(r, lp):
        return remote(
            own.at[lp], gathered.at[segment], e_send.at[r, lp], e_recv.at[segment],
            tm=(tm + r) % tm_size, space=back_target(lp),
        )

    for r in range(tm_size):
        for lp in range(2):
            if r == 0 and lp == 0:

                @pl.when(far)
                def _():
                    give_end(0, 0).start()

                @pl.when(near)
                def _():
                    pltpu.make_async_copy(
                        own.at[0], gathered.at[segment], e_recv.at[segment]
                    ).start()
            else:
                give_end(r, lp).start()
    for s in range(segments):
        arrived(gathered.at[s], e_recv.at[s])

    def ends(back):
        return [gathered[(2 * tm + segments - back) % segments, i] for i in range(SWEEPS)]

    def enter(back):
        entered = (2 * tm - back + 1 + segments) % segments
        return jnp.where(entered == 0, jnp.float32(WRAP_WEIGHT), jnp.float32(1.0))

    total = [enter(segments) * value for value in ends(segments)]
    for back in range(segments - 1, 0, -1):
        moved = advance(total)
        total = [enter(back) * (a + b) for a, b in zip(ends(back), moved)]
    start = [None] * SWEEPS
    for i in reversed(range(SWEEPS)):
        value = total[i]
        for j in range(i + 1, SWEEPS):
            value = value + WRAP_WEIGHT * around[i][j : j + 1, :] * start[j]
        start[i] = value / (1.0 - WRAP_WEIGHT * around[i][i : i + 1, :])
    later = [a + b for a, b in zip(ends(segments), advance(start))]
    for e in range(plane):
        for i in range(SWEEPS):
            start_ref[e, i : i + 1, :] = start[i][e : e + 1, :]
            start_ref[e, SWEEPS + i : SWEEPS + i + 1, :] = later[i][e : e + 1, :]

    save_table.wait()
    for k in range(CHUNKS):
        first, width = spans[k]
        for h in range(2):
            arrived(series_ref.at[:, pl.ds(h * half + first, width), :], r_recv.at[k, h])
    out_near().wait_send()
    for k in range(CHUNKS):
        out_data(k).wait_send()
        give_back(k, 1).wait_send()
        for j in range(moves):
            for d in range(2):
                transfer(j, k, d).wait_send()
    for r in range(tm_size):
        for lp in range(2):
            if r or lp:
                give_end(r, lp).wait_send()

    @pl.when(near)
    def _():
        for e in range(plane):
            @pl.when(tm == owner[e])
            def _():
                for lp in range(2):
                    out_blocks(lp, e).wait_send()

    @pl.when(far)
    def _():
        mate_near().wait_send()
        give_end(0, 0).wait_send()
        for k in range(CHUNKS):
            mate_data(k).wait_send()
            give_back(k, 0).wait_send()
        for e in range(plane):
            mate_blocks(e).wait_send()
            for lp in range(2):
                forwards(lp, e, lambda copy: copy.wait_send())


def finish(series_ref, table_ref, start_ref, out_ref):
    half = series_ref.shape[1] // 2

    def some(g, _):
        rows = pl.ds(pl.multiple_of(g * 4 * ROWS, 4 * ROWS), 4 * ROWS)
        lines = [table_ref[i, rows, :] for i in range(SWEEPS)]
        for h in range(2):
            place = pl.ds(pl.multiple_of(h * half + g * 4 * ROWS, 4 * ROWS), 4 * ROWS)
            for e in range(series_ref.shape[0]):
                value = series_ref[e, place, :]
                for i in range(SWEEPS):
                    row = h * SWEEPS + i
                    value = value + lines[i] * start_ref[e, row : row + 1, :]
                out_ref[e, place, :] = value
        return 0

    lax.fori_loop(0, half // (4 * ROWS), some, 0)


def solution(mesh):
    tm_size, sp_size = mesh.shape["tm"], mesh.shape["space"]

    def per_device(right_side, blocks, neighbors, shift_rates):
        plane, steps, nodes = right_side.shape
        half = steps // 2
        moves = SWEEPS - 1
        f32 = jnp.float32
        dma = pltpu.SemaphoreType.DMA
        whole = pltpu.VMEM((2, plane, half, nodes), f32)
        widths = [width for _, width in windows(half)]
        series, table, start = pl.pallas_call(
            functools.partial(kernel, tm_size, sp_size),
            out_shape=(
                jax.ShapeDtypeStruct(right_side.shape, f32),
                jax.ShapeDtypeStruct((SWEEPS, half, nodes), f32),
                jax.ShapeDtypeStruct((plane, 2 * SWEEPS, nodes), f32),
            ),
            in_specs=[
                pl.BlockSpec(memory_space=pl.ANY),
                pl.BlockSpec(memory_space=pl.ANY),
                pl.BlockSpec(memory_space=pl.ANY),
                pl.BlockSpec(memory_space=pltpu.SMEM),
            ],
            out_specs=(
                pl.BlockSpec(memory_space=pl.ANY),
                pl.BlockSpec(memory_space=pl.ANY),
                pl.BlockSpec(memory_space=pltpu.VMEM),
            ),
            scratch_shapes=[pltpu.VMEM((2, plane, width, nodes), f32) for width in widths]
            + [
                pltpu.VMEM((plane, width, nodes), f32)
                for _ in range(moves) for width in widths for _ in range(2)
            ]
            + [
                whole, whole, whole, whole,
                pltpu.VMEM((2,) + blocks.shape, f32),
                pltpu.VMEM((2, plane, SLOTS * nodes, 2 * nodes), jnp.bfloat16),
                pltpu.VMEM((SWEEPS, half, nodes), f32),
                pltpu.VMEM((2 * tm_size, SWEEPS, plane, nodes), f32),
                pltpu.VMEM((2, SWEEPS, plane, nodes), f32),
                pltpu.VMEM((2,) + neighbors.shape, jnp.int32),
                pltpu.SMEM((2,) + neighbors.shape, jnp.int32),
                dma((2, plane)),
                dma((2, plane)),
                dma((plane,)),
                dma((2, plane, 2)),
                dma((CHUNKS, 2)),
                dma((CHUNKS,)),
                dma((CHUNKS,)),
                dma((2,)),
                dma((2,)),
                dma((1,)),
                dma((moves, CHUNKS, 2)),
                dma((moves, CHUNKS, 2)),
                dma((CHUNKS, 2)),
                dma((CHUNKS, 2)),
                dma((tm_size, 2)),
                dma((2 * tm_size,)),
                dma((1,)),
            ],
            compiler_params=pltpu.CompilerParams(
                collective_id=0, has_side_effects=True, vmem_limit_bytes=60 * 2**20
            ),
        )(right_side, blocks, neighbors, shift_rates)
        block = pl.BlockSpec((2, steps, nodes), lambda e: (e, 0, 0))
        return pl.pallas_call(
            finish,
            grid=(plane // 2,),
            out_shape=jax.ShapeDtypeStruct(right_side.shape, f32),
            in_specs=[
                block,
                pl.BlockSpec((SWEEPS, half, nodes), lambda e: (0, 0, 0)),
                pl.BlockSpec((2, 2 * SWEEPS, nodes), lambda e: (e, 0, 0)),
            ],
            out_specs=block,
        )(series, table, start)

    return jax.shard_map(
        per_device,
        mesh=mesh,
        in_specs=(P("space", "tm", None), P("space", None, None, None), P("space", None), P()),
        out_specs=P("space", "tm", None),
        check_vma=False,
    )
```

```python
import functools

import jax
import jax.numpy as jnp
from jax import lax
from jax.experimental import pallas as pl
from jax.experimental.pallas import tpu as pltpu
from jax.sharding import PartitionSpec as P

SWEEPS = 4
SLOTS = 7
PIECES = (2, 2, 2, 2)
CHUNKS = len(PIECES)
ROWS = 8
WRAP_WEIGHT = 0.01
DIAG_WEIGHT = 6.0
BLOCK_WEIGHT = 3.0
STEP_SCALE = 0.1
MESH = pl.DeviceIdType.MESH


def split(value):
    hi = value.astype(jnp.bfloat16)
    lo = (value - hi.astype(jnp.float32)).astype(jnp.bfloat16)
    return hi, lo


def windows(half):
    unit = half // sum(PIECES)
    return [(unit * sum(PIECES[:c]), unit * PIECES[c]) for c in range(CHUNKS)]


def shares(plane):
    ends = (3 * plane) // 8
    rest = plane - ends
    kinds = []
    for lp in range(2):
        low = (rest + 1 - lp) // 2
        kinds.append([0] * ends + [1] * low + [2] * (rest - low))
    return kinds


def woven(kinds, lp):
    ends = [(lp, e) for e in range(len(kinds)) if kinds[e] == 0]
    low = [(lp, e) for e in range(len(kinds)) if kinds[e] == 1]
    high = [(lp, e) for e in range(len(kinds)) if kinds[e] == 2]
    middles = []
    while low or high:
        for side in (low, high) if lp == 0 else (high, low):
            if side:
                middles.append(side.pop(0))
    order = list(middles[: 2 - lp])
    for at, item in enumerate(ends):
        order.append(item)
        order += middles[2 - lp + at : 3 - lp + at]
    order += middles[2 - lp + len(ends) :]
    return middles, order


def kernel(
    tm_size, sp_size, x_ref, blocks_ref, near_ref, shift_ref,
    series_ref, table_ref, start_ref, *scratch
):
    plane, steps, nodes = x_ref.shape
    half = steps // 2
    spans = windows(half)
    moves = SWEEPS - 1
    groups = sp_size // 4
    segments = 2 * tm_size
    first_z = scratch[:CHUNKS]
    halos = scratch[CHUNKS : CHUNKS + 2 * moves * CHUNKS]
    (z1, z2, z3, series, held, weights, table, gathered, own, nearv, nears,
     w_recv, w_out, w_mate, w_fwd, d_recv, d_mate, d_out, n_recv, n_send, n_load,
     h_send, h_recv, r_send, r_recv, e_send, e_recv, t_store) = scratch[
        CHUNKS + 2 * moves * CHUNKS :
    ]
    zs = [None, z1, z2, z3]
    kinds = shares(plane)
    quad = tm_size % 4 == 0
    tm = lax.axis_index("tm")
    sp = lax.axis_index("space")
    group = sp // 4
    chip = (sp // 2) % 2
    core = sp % 2
    far_side = (chip + core) % 2
    far = far_side == 1
    near = far_side == 0
    layer = tm % 4 if quad else tm * 0
    middle = (layer == 1) | (layer == 2)
    end = (layer == 0) | (layer == 3)
    mate = group * 4 + chip * 2 + (1 - core)
    here_near = group * 4 + chip * 2 + chip
    there_far = group * 4 + (1 - chip) * 2 + chip
    across = ((group + groups + 2 * core - 1) % groups) * 4 + chip * 2 + (1 - core)

    def remote(src, dst, send, recv, **device):
        return pltpu.make_async_remote_copy(
            src_ref=src, dst_ref=dst, send_sem=send, recv_sem=recv,
            device_id=device, device_id_type=MESH,
        )

    def arrived(dst, recv):
        remote(dst, dst, n_send.at[0], recv, space=mate).wait_recv()

    barrier = pltpu.get_barrier_semaphore()
    greeted = 0
    for r in range(tm_size):
        for d in range(4):
            if r == 0 and d == 0:
                continue
            pl.semaphore_signal(
                barrier, inc=1, device_id_type=MESH,
                device_id={"tm": (tm + r) % tm_size, "space": group * 4 + (sp + d) % 4},
            )
            greeted += 1
    if groups > 1:
        pl.semaphore_signal(barrier, inc=1, device_id={"space": across}, device_id_type=MESH)
        greeted += 1

    def fetches(lp, e):
        if not quad or kinds[lp][e] == 0:
            return end
        return layer == kinds[lp][e]

    def own_load(e):
        return pltpu.make_async_copy(blocks_ref.at[e], held.at[0, e], w_recv.at[0, e])

    def own_data(k):
        first, width = spans[k]
        return pltpu.make_async_copy(
            x_ref.at[:, pl.ds(chip * half + first, width), :], first_z[k].at[0], d_recv.at[k, 0]
        )

    def mate_data(k):
        first, width = spans[k]
        return remote(
            x_ref.at[:, pl.ds(chip * half + first, width), :], first_z[k].at[1],
            d_mate.at[k], d_recv.at[k, 1], space=mate,
        )

    def out_data(k):
        first, width = spans[k]
        return remote(
            x_ref.at[:, pl.ds((1 - chip) * half + first, width), :], first_z[k].at[far_side],
            d_out.at[k], d_recv.at[k, far_side], space=there_far,
        )

    def out_blocks(lp, e):
        return remote(
            blocks_ref.at[e] if lp == 0 else held.at[1, e], held.at[lp, e],
            w_out.at[lp, e], w_recv.at[lp, e], space=there_far,
        )

    def mate_blocks(e):
        return remote(
            blocks_ref.at[e], held.at[1, e], w_mate.at[e], w_recv.at[1, e], space=mate
        )

    def out_near():
        return remote(
            near_ref, nearv.at[far_side], n_send.at[0], n_recv.at[far_side], space=there_far
        )

    def mate_near():
        return remote(near_ref, nearv.at[1], n_send.at[1], n_recv.at[1], space=mate)

    def forward(lp, e, up):
        return remote(
            held.at[lp, e], held.at[lp, e], w_fwd.at[lp, e, up], w_recv.at[lp, e],
            tm=tm + 1 if up else tm - 1,
        )

    def forwards(lp, e, act):
        if not quad:
            return
        downs, ups = (((3,), (0,)), ((1,), (1, 2)), ((2, 1), (2,)))[kinds[lp][e]]
        for way, layers in ((0, downs), (1, ups)):
            for at in layers:

                @pl.when(layer == at)
                def _():
                    act(forward(lp, e, way))

    def halo(j, k, d):
        return halos[(j * CHUNKS + k) * 2 + d]

    def part(j, k, lp):
        if j == 0:
            return first_z[k].at[lp]
        return zs[j].at[lp, :, pl.ds(*spans[k]), :]

    def transfer(j, k, d):
        return remote(
            part(j, k, d), halo(j, k, d), h_send.at[j, k, d], h_recv.at[j, k, d],
            space=across if d == 0 else mate,
        )

    @pl.when(near)
    def _():
        for e in range(plane):
            own_load(e).start()
        for k in range(CHUNKS):
            own_data(k).start()
        pltpu.make_async_copy(near_ref, nearv.at[0], n_recv.at[0]).start()

    pl.semaphore_wait(barrier, greeted)

    out_near().start()

    @pl.when(end)
    def _():
        for k in range(CHUNKS):
            out_data(k).start()

    @pl.when(near)
    def _():
        for e in range(plane):

            @pl.when(fetches(0, e))
            def _():
                out_blocks(0, e).start()

    @pl.when(far)
    def _():
        mate_near().start()
        for k in range(CHUNKS):
            mate_data(k).start()
        for e in range(plane):
            mate_blocks(e).start()

    sigmas = [STEP_SCALE * shift_ref[i] for i in range(SWEEPS)]
    rates = [1.0 / (1.0 + jnp.full((ROWS, nodes), sigma, jnp.float32)) for sigma in sigmas]

    def cascade(inputs, states):
        states = list(states)
        above = None
        for i in reversed(range(SWEEPS)):
            total = states[i] if inputs is None else inputs[i] + states[i]
            if above is not None:
                total = total + above
            states[i] = above = rates[i] * total
        return states

    row = lax.broadcasted_iota(jnp.int32, (ROWS, nodes), 0)
    unit = [(row == i).astype(jnp.float32) for i in range(SWEEPS)]

    def respond(g, states):
        kept = []
        for _ in range(ROWS):
            states = cascade(None, states)
            kept.append(states[0])
        flat = jnp.swapaxes(jnp.stack(kept), 0, 1)
        base = pl.multiple_of(g * ROWS, ROWS)
        for j in range(SWEEPS):
            table[j, pl.ds(base, ROWS), :] = flat[j]
        return tuple(states)

    over = lax.fori_loop(0, half // ROWS, respond, tuple(unit))
    save_table = pltpu.make_async_copy(table, table_ref, t_store.at[0])
    save_table.start()
    carry_of = [[over[i][j : j + 1, :] for j in range(SWEEPS)] for i in range(SWEEPS)]

    def advance(vectors):
        result = []
        for i in range(SWEEPS):
            total = carry_of[i][i] * vectors[i]
            for j in range(i + 1, SWEEPS):
                total = total + carry_of[i][j] * vectors[j]
            result.append(total)
        return result

    around = list(over)
    for _ in range(segments - 1):
        around = advance(around)

    def prepare(lp, e):
        outer_slot = 1 + (core if lp == 0 else 1 - core)
        for b in range(SLOTS):
            s = outer_slot if b == 1 else 3 - outer_slot if b == 2 else b
            hi, lo = split((-STEP_SCALE * BLOCK_WEIGHT) * held[lp, e, s].T)
            weights[lp, e, b * nodes : (b + 1) * nodes, :nodes] = hi
            weights[lp, e, b * nodes : (b + 1) * nodes, nodes:] = lo

    def prepare_all(lp):
        def one(e, _):
            prepare(lp, e)
            return 0

        lax.fori_loop(0, plane, one, 0)

    @pl.when(near)
    def _():
        for e in range(plane):
            arrived(held.at[1, e], w_recv.at[1, e])

            @pl.when(fetches(1, e))
            def _():
                out_blocks(1, e).start()

        @pl.when(middle)
        def _():
            for k in range(CHUNKS):
                out_data(k).start()

        for k in range(CHUNKS):
            for lp in range(2):
                arrived(first_z[k].at[lp], d_recv.at[k, lp])
                transfer(0, k, lp).start()
        for e in range(plane):
            own_load(e).wait()
        prepare_all(0)
        prepare_all(1)

    def receive(lp, e):
        arrived(held.at[lp, e], w_recv.at[lp, e])
        forwards(lp, e, lambda copy: copy.start())
        prepare(lp, e)

    between = [woven(kinds[lp], lp) for lp in range(2)]

    @pl.when(far & middle)
    def _():
        ahead = between[0][0] + between[1][0]
        for i, item in enumerate(ahead):
            receive(*item)
            if i == min(6, len(ahead) - 1):
                for k in range(CHUNKS):
                    out_data(k).start()

    @pl.when(far)
    def _():
        for k in range(CHUNKS):
            for lp in range(2):
                arrived(first_z[k].at[lp], d_recv.at[k, lp])
                transfer(0, k, lp).start()

    def receive_all(lp):
        for _, e in between[lp][1]:

            @pl.when(far & (end if kinds[lp][e] else layer >= 0))
            def _():
                receive(lp, e)

    receive_all(0)

    for lp in range(2):
        arrived(nearv.at[lp], n_recv.at[lp])
    load_near = pltpu.make_async_copy(nearv, nears, n_load.at[0])
    load_near.start()
    load_near.wait()

    def apply(j, k, lp):
        first, width = spans[k]
        window = pl.ds(first, width)
        diag = sigmas[j] - STEP_SCALE * DIAG_WEIGHT
        outer_slot = 1 + (core if lp == 0 else 1 - core)

        def source(q, index):
            return first_z[k][q, index] if j == 0 else zs[j][q, index, window, :]

        def one(e, _):
            def near_of(s):
                return lax.rem(nears[lp, e, s], plane)

            here = source(lp, e)
            parts = [
                here,
                halo(j, k, lp)[near_of(outer_slot)],
                source(1 - lp, near_of(3 - outer_slot)),
            ] + [source(lp, near_of(s)) for s in range(3, SLOTS)]
            pairs = [split(p) for p in parts]
            hi = jnp.concatenate([p[0] for p in pairs], axis=1)
            lo = jnp.concatenate([p[1] for p in pairs], axis=1)
            rows = jnp.concatenate([hi, lo], axis=0)
            both = jnp.dot(rows, weights[lp, e], preferred_element_type=jnp.float32)
            both = both[:width] + both[width:]
            zs[j + 1][lp, e, window, :] = diag * here + both[:, :nodes] + both[:, nodes:]
            return 0

        lax.fori_loop(0, plane, one, 0, unroll=4)

    for lp in range(2):
        if lp == 1:
            receive_all(1)
        for k in range(CHUNKS):
            transfer(0, k, lp).wait_recv()
            apply(0, k, lp)
            transfer(1, k, lp).start()

    for lp in range(2):
        for k in range(CHUNKS):
            transfer(1, k, lp).wait_recv()
            apply(1, k, lp)
            transfer(2, k, lp).start()

    def back_target(lp):
        return group * 4 + 2 * core + (core + lp) % 2

    def give_back(k, lp):
        first, width = spans[k]
        return remote(
            series.at[lp, :, pl.ds(first, width), :],
            series_ref.at[:, pl.ds(chip * half + first, width), :],
            r_send.at[k, lp], r_recv.at[k, chip], space=back_target(lp),
        )

    def keep_back(k):
        first, width = spans[k]
        return pltpu.make_async_copy(
            series.at[0, :, pl.ds(first, width), :],
            series_ref.at[:, pl.ds(chip * half + first, width), :],
            r_recv.at[k, chip],
        )

    states = tuple(jnp.zeros((ROWS, nodes), jnp.float32) for _ in range(2 * SWEEPS))
    for k in range(CHUNKS):
        first, width = spans[k]
        for lp in range(2):
            transfer(2, k, lp).wait_recv()
            apply(2, k, lp)

        def scan(g, states):
            states = list(states)
            base = pl.multiple_of(first + g * ROWS, ROWS)
            inner = pl.multiple_of(g * ROWS, ROWS)
            for lp in range(2):
                mine = states[lp * SWEEPS : (lp + 1) * SWEEPS]
                here = [jnp.swapaxes(first_z[k][lp, :, pl.ds(inner, ROWS), :], 0, 1)] + [
                    jnp.swapaxes(z[lp, :, pl.ds(base, ROWS), :], 0, 1) for z in zs[1:]
                ]
                kept = []
                for t in range(ROWS):
                    mine = cascade([h[t] for h in here], mine)
                    kept.append(mine[0])
                series[lp, :, pl.ds(base, ROWS), :] = jnp.swapaxes(jnp.stack(kept), 0, 1)
                states[lp * SWEEPS : (lp + 1) * SWEEPS] = mine
            return tuple(states)

        states = lax.fori_loop(0, width // ROWS, scan, states)
        give_back(k, 1).start()

        @pl.when(far)
        def _():
            give_back(k, 0).start()

        @pl.when(near)
        def _():
            keep_back(k).start()

    for lp in range(2):
        for i in range(SWEEPS):
            own[lp, i] = states[lp * SWEEPS + i]
    segment = 2 * tm + chip

    def give_end(r, lp):
        return remote(
            own.at[lp], gathered.at[segment], e_send.at[r, lp], e_recv.at[segment],
            tm=(tm + r) % tm_size, space=back_target(lp),
        )

    for r in range(tm_size):
        for lp in range(2):
            if r == 0 and lp == 0:

                @pl.when(far)
                def _():
                    give_end(0, 0).start()

                @pl.when(near)
                def _():
                    pltpu.make_async_copy(
                        own.at[0], gathered.at[segment], e_recv.at[segment]
                    ).start()
            else:
                give_end(r, lp).start()
    for s in range(segments):
        arrived(gathered.at[s], e_recv.at[s])

    def ends(back):
        return [gathered[(2 * tm + segments - back) % segments, i] for i in range(SWEEPS)]

    def enter(back):
        entered = (2 * tm - back + 1 + segments) % segments
        return jnp.where(entered == 0, jnp.float32(WRAP_WEIGHT), jnp.float32(1.0))

    total = [enter(segments) * value for value in ends(segments)]
    for back in range(segments - 1, 0, -1):
        moved = advance(total)
        total = [enter(back) * (a + b) for a, b in zip(ends(back), moved)]
    start = [None] * SWEEPS
    for i in reversed(range(SWEEPS)):
        value = total[i]
        for j in range(i + 1, SWEEPS):
            value = value + WRAP_WEIGHT * around[i][j : j + 1, :] * start[j]
        start[i] = value / (1.0 - WRAP_WEIGHT * around[i][i : i + 1, :])
    later = [a + b for a, b in zip(ends(segments), advance(start))]
    for e in range(plane):
        for i in range(SWEEPS):
            start_ref[e, i : i + 1, :] = start[i][e : e + 1, :]
            start_ref[e, SWEEPS + i : SWEEPS + i + 1, :] = later[i][e : e + 1, :]

    save_table.wait()
    for k in range(CHUNKS):
        first, width = spans[k]
        for h in range(2):
            arrived(series_ref.at[:, pl.ds(h * half + first, width), :], r_recv.at[k, h])
    out_near().wait_send()
    for k in range(CHUNKS):
        out_data(k).wait_send()
        give_back(k, 1).wait_send()
        for j in range(moves):
            for d in range(2):
                transfer(j, k, d).wait_send()
    for r in range(tm_size):
        for lp in range(2):
            if r or lp:
                give_end(r, lp).wait_send()

    @pl.when(near)
    def _():
        for e in range(plane):
            for lp in range(2):

                @pl.when(fetches(lp, e))
                def _():
                    out_blocks(lp, e).wait_send()

    @pl.when(far)
    def _():
        mate_near().wait_send()
        give_end(0, 0).wait_send()
        for k in range(CHUNKS):
            mate_data(k).wait_send()
            give_back(k, 0).wait_send()
        for e in range(plane):
            mate_blocks(e).wait_send()
            for lp in range(2):
                forwards(lp, e, lambda copy: copy.wait_send())


def finish(series_ref, table_ref, start_ref, out_ref):
    half = series_ref.shape[1] // 2

    def some(g, _):
        rows = pl.ds(pl.multiple_of(g * 4 * ROWS, 4 * ROWS), 4 * ROWS)
        lines = [table_ref[i, rows, :] for i in range(SWEEPS)]
        for h in range(2):
            place = pl.ds(pl.multiple_of(h * half + g * 4 * ROWS, 4 * ROWS), 4 * ROWS)
            for e in range(series_ref.shape[0]):
                value = series_ref[e, place, :]
                for i in range(SWEEPS):
                    row = h * SWEEPS + i
                    value = value + lines[i] * start_ref[e, row : row + 1, :]
                out_ref[e, place, :] = value
        return 0

    lax.fori_loop(0, half // (4 * ROWS), some, 0)


def solution(mesh):
    tm_size, sp_size = mesh.shape["tm"], mesh.shape["space"]

    def per_device(right_side, blocks, neighbors, shift_rates):
        plane, steps, nodes = right_side.shape
        half = steps // 2
        moves = SWEEPS - 1
        f32 = jnp.float32
        dma = pltpu.SemaphoreType.DMA
        whole = pltpu.VMEM((2, plane, half, nodes), f32)
        widths = [width for _, width in windows(half)]
        series, table, start = pl.pallas_call(
            functools.partial(kernel, tm_size, sp_size),
            out_shape=(
                jax.ShapeDtypeStruct(right_side.shape, f32),
                jax.ShapeDtypeStruct((SWEEPS, half, nodes), f32),
                jax.ShapeDtypeStruct((plane, 2 * SWEEPS, nodes), f32),
            ),
            in_specs=[
                pl.BlockSpec(memory_space=pl.ANY),
                pl.BlockSpec(memory_space=pl.ANY),
                pl.BlockSpec(memory_space=pl.ANY),
                pl.BlockSpec(memory_space=pltpu.SMEM),
            ],
            out_specs=(
                pl.BlockSpec(memory_space=pl.ANY),
                pl.BlockSpec(memory_space=pl.ANY),
                pl.BlockSpec(memory_space=pltpu.VMEM),
            ),
            scratch_shapes=[pltpu.VMEM((2, plane, width, nodes), f32) for width in widths]
            + [
                pltpu.VMEM((plane, width, nodes), f32)
                for _ in range(moves) for width in widths for _ in range(2)
            ]
            + [
                whole, whole, whole, whole,
                pltpu.VMEM((2,) + blocks.shape, f32),
                pltpu.VMEM((2, plane, SLOTS * nodes, 2 * nodes), jnp.bfloat16),
                pltpu.VMEM((SWEEPS, half, nodes), f32),
                pltpu.VMEM((2 * tm_size, SWEEPS, plane, nodes), f32),
                pltpu.VMEM((2, SWEEPS, plane, nodes), f32),
                pltpu.VMEM((2,) + neighbors.shape, jnp.int32),
                pltpu.SMEM((2,) + neighbors.shape, jnp.int32),
                dma((2, plane)),
                dma((2, plane)),
                dma((plane,)),
                dma((2, plane, 2)),
                dma((CHUNKS, 2)),
                dma((CHUNKS,)),
                dma((CHUNKS,)),
                dma((2,)),
                dma((2,)),
                dma((1,)),
                dma((moves, CHUNKS, 2)),
                dma((moves, CHUNKS, 2)),
                dma((CHUNKS, 2)),
                dma((CHUNKS, 2)),
                dma((tm_size, 2)),
                dma((2 * tm_size,)),
                dma((1,)),
            ],
            compiler_params=pltpu.CompilerParams(
                collective_id=0, has_side_effects=True, vmem_limit_bytes=60 * 2**20
            ),
        )(right_side, blocks, neighbors, shift_rates)
        block = pl.BlockSpec((2, steps, nodes), lambda e: (e, 0, 0))
        return pl.pallas_call(
            finish,
            grid=(plane // 2,),
            out_shape=jax.ShapeDtypeStruct(right_side.shape, f32),
            in_specs=[
                block,
                pl.BlockSpec((SWEEPS, half, nodes), lambda e: (0, 0, 0)),
                pl.BlockSpec((2, 2 * SWEEPS, nodes), lambda e: (e, 0, 0)),
            ],
            out_specs=block,
        )(series, table, start)

    return jax.shard_map(
        per_device,
        mesh=mesh,
        in_specs=(P("space", "tm", None), P("space", None, None, None), P("space", None), P()),
        out_specs=P("space", "tm", None),
        check_vma=False,
    )
```

```python
import functools

import jax
import jax.numpy as jnp
from jax import lax
from jax.experimental import pallas as pl
from jax.experimental.pallas import tpu as pltpu
from jax.sharding import PartitionSpec as P

SWEEPS = 4
SLOTS = 7
PIECES = (2, 2, 2, 2)
CHUNKS = len(PIECES)
ROWS = 8
WRAP_WEIGHT = 0.01
DIAG_WEIGHT = 6.0
BLOCK_WEIGHT = 3.0
STEP_SCALE = 0.1
MESH = pl.DeviceIdType.MESH


def split(value):
    hi = value.astype(jnp.bfloat16)
    lo = (value - hi.astype(jnp.float32)).astype(jnp.bfloat16)
    return hi, lo


def windows(half):
    unit = half // sum(PIECES)
    return [(unit * sum(PIECES[:c]), unit * PIECES[c]) for c in range(CHUNKS)]


def shares(plane):
    ends = (3 * plane) // 8
    rest = plane - ends
    kinds = []
    for lp in range(2):
        low = (rest + 1 - lp) // 2
        kinds.append([0] * ends + [1] * low + [2] * (rest - low))
    return kinds


def woven(kinds, lp):
    ends = [(lp, e) for e in range(len(kinds)) if kinds[e] == 0]
    low = [(lp, e) for e in range(len(kinds)) if kinds[e] == 1]
    high = [(lp, e) for e in range(len(kinds)) if kinds[e] == 2]
    middles = []
    while low or high:
        for side in (low, high) if lp == 0 else (high, low):
            if side:
                middles.append(side.pop(0))
    order = list(middles[: 2 - lp])
    for at, item in enumerate(ends):
        order.append(item)
        order += middles[2 - lp + at : 3 - lp + at]
    order += middles[2 - lp + len(ends) :]
    return middles, order


def kernel(
    tm_size, sp_size, x_ref, blocks_ref, near_ref, shift_ref,
    series_ref, table_ref, start_ref, *scratch
):
    plane, steps, nodes = x_ref.shape
    half = steps // 2
    spans = windows(half)
    moves = SWEEPS - 1
    groups = sp_size // 4
    segments = 2 * tm_size
    first_z = scratch[:CHUNKS]
    halos = scratch[CHUNKS : CHUNKS + 2 * moves * CHUNKS]
    (z1, z2, z3, series, held, weights, table, gathered, own, nearv, nears,
     w_recv, w_out, w_mate, w_fwd, d_recv, d_mate, d_out, n_recv, n_send, n_load,
     h_send, h_recv, r_send, r_recv, e_send, e_recv, t_store) = scratch[
        CHUNKS + 2 * moves * CHUNKS :
    ]
    zs = [None, z1, z2, z3]
    kinds = shares(plane)
    quad = tm_size % 4 == 0
    tm = lax.axis_index("tm")
    sp = lax.axis_index("space")
    group = sp // 4
    chip = (sp // 2) % 2
    core = sp % 2
    far_side = (chip + core) % 2
    far = far_side == 1
    near = far_side == 0
    layer = tm % 4 if quad else tm * 0
    middle = (layer == 1) | (layer == 2)
    end = (layer == 0) | (layer == 3)
    mate = group * 4 + chip * 2 + (1 - core)
    here_near = group * 4 + chip * 2 + chip
    there_far = group * 4 + (1 - chip) * 2 + chip
    across = ((group + groups + 2 * core - 1) % groups) * 4 + chip * 2 + (1 - core)

    def remote(src, dst, send, recv, **device):
        return pltpu.make_async_remote_copy(
            src_ref=src, dst_ref=dst, send_sem=send, recv_sem=recv,
            device_id=device, device_id_type=MESH,
        )

    def arrived(dst, recv):
        remote(dst, dst, n_send.at[0], recv, space=mate).wait_recv()

    barrier = pltpu.get_barrier_semaphore()
    greeted = 0
    for r in range(tm_size):
        for d in range(4):
            if r == 0 and d == 0:
                continue
            pl.semaphore_signal(
                barrier, inc=1, device_id_type=MESH,
                device_id={"tm": (tm + r) % tm_size, "space": group * 4 + (sp + d) % 4},
            )
            greeted += 1
    if groups > 1:
        pl.semaphore_signal(barrier, inc=1, device_id={"space": across}, device_id_type=MESH)
        greeted += 1

    def fetches(lp, e):
        if not quad or kinds[lp][e] == 0:
            return end
        return layer == kinds[lp][e]

    def own_load(e):
        return pltpu.make_async_copy(blocks_ref.at[e], held.at[0, e], w_recv.at[0, e])

    def own_data(k):
        first, width = spans[k]
        return pltpu.make_async_copy(
            x_ref.at[:, pl.ds(chip * half + first, width), :], first_z[k].at[0], d_recv.at[k, 0]
        )

    def mate_data(k):
        first, width = spans[k]
        return remote(
            x_ref.at[:, pl.ds(chip * half + first, width), :], first_z[k].at[1],
            d_mate.at[k], d_recv.at[k, 1], space=mate,
        )

    def out_data(k):
        first, width = spans[k]
        return remote(
            x_ref.at[:, pl.ds((1 - chip) * half + first, width), :], first_z[k].at[far_side],
            d_out.at[k], d_recv.at[k, far_side], space=there_far,
        )

    def out_blocks(lp, e):
        return remote(
            blocks_ref.at[e] if lp == 0 else held.at[1, e], held.at[lp, e],
            w_out.at[lp, e], w_recv.at[lp, e], space=there_far,
        )

    def mate_blocks(e):
        return remote(
            blocks_ref.at[e], held.at[1, e], w_mate.at[e], w_recv.at[1, e], space=mate
        )

    def out_near():
        return remote(
            near_ref, nearv.at[far_side], n_send.at[0], n_recv.at[far_side], space=there_far
        )

    def mate_near():
        return remote(near_ref, nearv.at[1], n_send.at[1], n_recv.at[1], space=mate)

    def forward(lp, e, up):
        return remote(
            held.at[lp, e], held.at[lp, e], w_fwd.at[lp, e, up], w_recv.at[lp, e],
            tm=tm + 1 if up else tm - 1,
        )

    def forwards(lp, e, act):
        if not quad:
            return
        downs, ups = (((3,), (0,)), ((1,), (1, 2)), ((2, 1), (2,)))[kinds[lp][e]]
        for way, layers in ((0, downs), (1, ups)):
            for at in layers:

                @pl.when(layer == at)
                def _():
                    act(forward(lp, e, way))

    def halo(j, k, d):
        return halos[(j * CHUNKS + k) * 2 + d]

    def part(j, k, lp):
        if j == 0:
            return first_z[k].at[lp]
        return zs[j].at[lp, :, pl.ds(*spans[k]), :]

    def transfer(j, k, d):
        return remote(
            part(j, k, d), halo(j, k, d), h_send.at[j, k, d], h_recv.at[j, k, d],
            space=across if d == 0 else mate,
        )

    @pl.when(near)
    def _():
        for e in range(plane):
            own_load(e).start()
        for k in range(CHUNKS):
            own_data(k).start()
        pltpu.make_async_copy(near_ref, nearv.at[0], n_recv.at[0]).start()

    pl.semaphore_wait(barrier, greeted)

    out_near().start()

    @pl.when(end)
    def _():
        for k in range(CHUNKS):
            out_data(k).start()

    @pl.when(near)
    def _():
        for e in range(plane):

            @pl.when(fetches(0, e))
            def _():
                out_blocks(0, e).start()

    @pl.when(far)
    def _():
        mate_near().start()
        for k in range(CHUNKS):
            mate_data(k).start()
        for e in range(plane):
            mate_blocks(e).start()

    sigmas = [STEP_SCALE * shift_ref[i] for i in range(SWEEPS)]
    rates = [1.0 / (1.0 + jnp.full((ROWS, nodes), sigma, jnp.float32)) for sigma in sigmas]

    def cascade(inputs, states):
        states = list(states)
        above = None
        for i in reversed(range(SWEEPS)):
            total = states[i] if inputs is None else inputs[i] + states[i]
            if above is not None:
                total = total + above
            states[i] = above = rates[i] * total
        return states

    row = lax.broadcasted_iota(jnp.int32, (ROWS, nodes), 0)
    unit = [(row == i).astype(jnp.float32) for i in range(SWEEPS)]

    def respond(g, states):
        kept = []
        for _ in range(ROWS):
            states = cascade(None, states)
            kept.append(states[0])
        flat = jnp.swapaxes(jnp.stack(kept), 0, 1)
        base = pl.multiple_of(g * ROWS, ROWS)
        for j in range(SWEEPS):
            table[j, pl.ds(base, ROWS), :] = flat[j]
        return tuple(states)

    over = lax.fori_loop(0, half // ROWS, respond, tuple(unit))
    save_table = pltpu.make_async_copy(table, table_ref, t_store.at[0])
    save_table.start()
    carry_of = [[over[i][j : j + 1, :] for j in range(SWEEPS)] for i in range(SWEEPS)]

    def advance(vectors):
        result = []
        for i in range(SWEEPS):
            total = carry_of[i][i] * vectors[i]
            for j in range(i + 1, SWEEPS):
                total = total + carry_of[i][j] * vectors[j]
            result.append(total)
        return result

    around = list(over)
    for _ in range(segments - 1):
        around = advance(around)

    def prepare(lp, e):
        outer_slot = 1 + (core if lp == 0 else 1 - core)
        for b in range(SLOTS):
            s = outer_slot if b == 1 else 3 - outer_slot if b == 2 else b
            hi, lo = split((-STEP_SCALE * BLOCK_WEIGHT) * held[lp, e, s].T)
            weights[lp, e, b * nodes : (b + 1) * nodes, :nodes] = hi
            weights[lp, e, b * nodes : (b + 1) * nodes, nodes:] = lo

    def prepare_all(lp):
        def one(e, _):
            prepare(lp, e)
            return 0

        lax.fori_loop(0, plane, one, 0)

    @pl.when(near)
    def _():
        for e in range(plane):
            arrived(held.at[1, e], w_recv.at[1, e])

            @pl.when(fetches(1, e))
            def _():
                out_blocks(1, e).start()

        @pl.when(middle)
        def _():
            for k in range(CHUNKS):
                out_data(k).start()

        for k in range(CHUNKS):
            for lp in range(2):
                arrived(first_z[k].at[lp], d_recv.at[k, lp])
                transfer(0, k, lp).start()
        for e in range(plane):
            own_load(e).wait()
        prepare_all(0)
        prepare_all(1)

    def take(lp, e):
        arrived(held.at[lp, e], w_recv.at[lp, e])
        forwards(lp, e, lambda copy: copy.start())

    between = [woven(kinds[lp], lp) for lp in range(2)]
    ends = sum(kind == 0 for kind in kinds[0])
    for side in (1, 2):

        @pl.when(far & (layer == side))
        def _():
            mine = [(lp, e) for lp in range(2) for e in range(plane) if kinds[lp][e] == side]
            theirs = [(lp, e) for lp in range(2) for e in range(plane) if kinds[lp][e] == 3 - side]
            for i in range(max(len(mine), len(theirs) + 2)):
                if i < len(mine):
                    take(*mine[i])
                if i == len(mine) - 1:
                    for k in range(CHUNKS):
                        out_data(k).start()
                if 0 <= i - 1 < len(theirs):
                    take(*theirs[i - 1])

    @pl.when(far & middle)
    def _():
        for lp in range(2):

            def one(e, _):
                prepare(lp, e)
                return 0

            lax.fori_loop(ends, plane, one, 0)

    @pl.when(far)
    def _():
        for k in range(CHUNKS):
            for lp in range(2):
                arrived(first_z[k].at[lp], d_recv.at[k, lp])
                transfer(0, k, lp).start()

    def receive_all(lp):
        for _, e in between[lp][1]:

            @pl.when(far & (end if kinds[lp][e] else layer >= 0))
            def _():
                take(lp, e)
                prepare(lp, e)

    receive_all(0)

    for lp in range(2):
        arrived(nearv.at[lp], n_recv.at[lp])
    load_near = pltpu.make_async_copy(nearv, nears, n_load.at[0])
    load_near.start()
    load_near.wait()

    def apply(j, k, lp):
        first, width = spans[k]
        window = pl.ds(first, width)
        diag = sigmas[j] - STEP_SCALE * DIAG_WEIGHT
        outer_slot = 1 + (core if lp == 0 else 1 - core)

        def source(q, index):
            return first_z[k][q, index] if j == 0 else zs[j][q, index, window, :]

        def one(e, _):
            def near_of(s):
                return lax.rem(nears[lp, e, s], plane)

            here = source(lp, e)
            parts = [
                here,
                halo(j, k, lp)[near_of(outer_slot)],
                source(1 - lp, near_of(3 - outer_slot)),
            ] + [source(lp, near_of(s)) for s in range(3, SLOTS)]
            pairs = [split(p) for p in parts]
            hi = jnp.concatenate([p[0] for p in pairs], axis=1)
            lo = jnp.concatenate([p[1] for p in pairs], axis=1)
            rows = jnp.concatenate([hi, lo], axis=0)
            both = jnp.dot(rows, weights[lp, e], preferred_element_type=jnp.float32)
            both = both[:width] + both[width:]
            zs[j + 1][lp, e, window, :] = diag * here + both[:, :nodes] + both[:, nodes:]
            return 0

        lax.fori_loop(0, plane, one, 0, unroll=4)

    for lp in range(2):
        if lp == 1:
            receive_all(1)
        for k in range(CHUNKS):
            transfer(0, k, lp).wait_recv()
            apply(0, k, lp)
            transfer(1, k, lp).start()

    for lp in range(2):
        for k in range(CHUNKS):
            transfer(1, k, lp).wait_recv()
            apply(1, k, lp)
            transfer(2, k, lp).start()

    def back_target(lp):
        return group * 4 + 2 * core + (core + lp) % 2

    def give_back(k, lp):
        first, width = spans[k]
        return remote(
            series.at[lp, :, pl.ds(first, width), :],
            series_ref.at[:, pl.ds(chip * half + first, width), :],
            r_send.at[k, lp], r_recv.at[k, chip], space=back_target(lp),
        )

    def keep_back(k):
        first, width = spans[k]
        return pltpu.make_async_copy(
            series.at[0, :, pl.ds(first, width), :],
            series_ref.at[:, pl.ds(chip * half + first, width), :],
            r_recv.at[k, chip],
        )

    states = tuple(jnp.zeros((ROWS, nodes), jnp.float32) for _ in range(2 * SWEEPS))
    for k in range(CHUNKS):
        first, width = spans[k]
        for lp in range(2):
            transfer(2, k, lp).wait_recv()
            apply(2, k, lp)

        def scan(g, states):
            states = list(states)
            base = pl.multiple_of(first + g * ROWS, ROWS)
            inner = pl.multiple_of(g * ROWS, ROWS)
            for lp in range(2):
                mine = states[lp * SWEEPS : (lp + 1) * SWEEPS]
                here = [jnp.swapaxes(first_z[k][lp, :, pl.ds(inner, ROWS), :], 0, 1)] + [
                    jnp.swapaxes(z[lp, :, pl.ds(base, ROWS), :], 0, 1) for z in zs[1:]
                ]
                kept = []
                for t in range(ROWS):
                    mine = cascade([h[t] for h in here], mine)
                    kept.append(mine[0])
                series[lp, :, pl.ds(base, ROWS), :] = jnp.swapaxes(jnp.stack(kept), 0, 1)
                states[lp * SWEEPS : (lp + 1) * SWEEPS] = mine
            return tuple(states)

        states = lax.fori_loop(0, width // ROWS, scan, states)
        give_back(k, 1).start()

        @pl.when(far)
        def _():
            give_back(k, 0).start()

        @pl.when(near)
        def _():
            keep_back(k).start()

    for lp in range(2):
        for i in range(SWEEPS):
            own[lp, i] = states[lp * SWEEPS + i]
    segment = 2 * tm + chip

    def give_end(r, lp):
        return remote(
            own.at[lp], gathered.at[segment], e_send.at[r, lp], e_recv.at[segment],
            tm=(tm + r) % tm_size, space=back_target(lp),
        )

    for r in range(tm_size):
        for lp in range(2):
            if r == 0 and lp == 0:

                @pl.when(far)
                def _():
                    give_end(0, 0).start()

                @pl.when(near)
                def _():
                    pltpu.make_async_copy(
                        own.at[0], gathered.at[segment], e_recv.at[segment]
                    ).start()
            else:
                give_end(r, lp).start()
    for s in range(segments):
        arrived(gathered.at[s], e_recv.at[s])

    def ends(back):
        return [gathered[(2 * tm + segments - back) % segments, i] for i in range(SWEEPS)]

    def enter(back):
        entered = (2 * tm - back + 1 + segments) % segments
        return jnp.where(entered == 0, jnp.float32(WRAP_WEIGHT), jnp.float32(1.0))

    total = [enter(segments) * value for value in ends(segments)]
    for back in range(segments - 1, 0, -1):
        moved = advance(total)
        total = [enter(back) * (a + b) for a, b in zip(ends(back), moved)]
    start = [None] * SWEEPS
    for i in reversed(range(SWEEPS)):
        value = total[i]
        for j in range(i + 1, SWEEPS):
            value = value + WRAP_WEIGHT * around[i][j : j + 1, :] * start[j]
        start[i] = value / (1.0 - WRAP_WEIGHT * around[i][i : i + 1, :])
    later = [a + b for a, b in zip(ends(segments), advance(start))]
    for e in range(plane):
        for i in range(SWEEPS):
            start_ref[e, i : i + 1, :] = start[i][e : e + 1, :]
            start_ref[e, SWEEPS + i : SWEEPS + i + 1, :] = later[i][e : e + 1, :]

    save_table.wait()
    for k in range(CHUNKS):
        first, width = spans[k]
        for h in range(2):
            arrived(series_ref.at[:, pl.ds(h * half + first, width), :], r_recv.at[k, h])
    out_near().wait_send()
    for k in range(CHUNKS):
        out_data(k).wait_send()
        give_back(k, 1).wait_send()
        for j in range(moves):
            for d in range(2):
                transfer(j, k, d).wait_send()
    for r in range(tm_size):
        for lp in range(2):
            if r or lp:
                give_end(r, lp).wait_send()

    @pl.when(near)
    def _():
        for e in range(plane):
            for lp in range(2):

                @pl.when(fetches(lp, e))
                def _():
                    out_blocks(lp, e).wait_send()

    @pl.when(far)
    def _():
        mate_near().wait_send()
        give_end(0, 0).wait_send()
        for k in range(CHUNKS):
            mate_data(k).wait_send()
            give_back(k, 0).wait_send()
        for e in range(plane):
            mate_blocks(e).wait_send()
            for lp in range(2):
                forwards(lp, e, lambda copy: copy.wait_send())


def finish(series_ref, table_ref, start_ref, out_ref):
    half = series_ref.shape[1] // 2

    def some(g, _):
        rows = pl.ds(pl.multiple_of(g * 4 * ROWS, 4 * ROWS), 4 * ROWS)
        lines = [table_ref[i, rows, :] for i in range(SWEEPS)]
        for h in range(2):
            place = pl.ds(pl.multiple_of(h * half + g * 4 * ROWS, 4 * ROWS), 4 * ROWS)
            for e in range(series_ref.shape[0]):
                value = series_ref[e, place, :]
                for i in range(SWEEPS):
                    row = h * SWEEPS + i
                    value = value + lines[i] * start_ref[e, row : row + 1, :]
                out_ref[e, place, :] = value
        return 0

    lax.fori_loop(0, half // (4 * ROWS), some, 0)


def solution(mesh):
    tm_size, sp_size = mesh.shape["tm"], mesh.shape["space"]

    def per_device(right_side, blocks, neighbors, shift_rates):
        plane, steps, nodes = right_side.shape
        half = steps // 2
        moves = SWEEPS - 1
        f32 = jnp.float32
        dma = pltpu.SemaphoreType.DMA
        whole = pltpu.VMEM((2, plane, half, nodes), f32)
        widths = [width for _, width in windows(half)]
        series, table, start = pl.pallas_call(
            functools.partial(kernel, tm_size, sp_size),
            out_shape=(
                jax.ShapeDtypeStruct(right_side.shape, f32),
                jax.ShapeDtypeStruct((SWEEPS, half, nodes), f32),
                jax.ShapeDtypeStruct((plane, 2 * SWEEPS, nodes), f32),
            ),
            in_specs=[
                pl.BlockSpec(memory_space=pl.ANY),
                pl.BlockSpec(memory_space=pl.ANY),
                pl.BlockSpec(memory_space=pl.ANY),
                pl.BlockSpec(memory_space=pltpu.SMEM),
            ],
            out_specs=(
                pl.BlockSpec(memory_space=pl.ANY),
                pl.BlockSpec(memory_space=pl.ANY),
                pl.BlockSpec(memory_space=pltpu.VMEM),
            ),
            scratch_shapes=[pltpu.VMEM((2, plane, width, nodes), f32) for width in widths]
            + [
                pltpu.VMEM((plane, width, nodes), f32)
                for _ in range(moves) for width in widths for _ in range(2)
            ]
            + [
                whole, whole, whole, whole,
                pltpu.VMEM((2,) + blocks.shape, f32),
                pltpu.VMEM((2, plane, SLOTS * nodes, 2 * nodes), jnp.bfloat16),
                pltpu.VMEM((SWEEPS, half, nodes), f32),
                pltpu.VMEM((2 * tm_size, SWEEPS, plane, nodes), f32),
                pltpu.VMEM((2, SWEEPS, plane, nodes), f32),
                pltpu.VMEM((2,) + neighbors.shape, jnp.int32),
                pltpu.SMEM((2,) + neighbors.shape, jnp.int32),
                dma((2, plane)),
                dma((2, plane)),
                dma((plane,)),
                dma((2, plane, 2)),
                dma((CHUNKS, 2)),
                dma((CHUNKS,)),
                dma((CHUNKS,)),
                dma((2,)),
                dma((2,)),
                dma((1,)),
                dma((moves, CHUNKS, 2)),
                dma((moves, CHUNKS, 2)),
                dma((CHUNKS, 2)),
                dma((CHUNKS, 2)),
                dma((tm_size, 2)),
                dma((2 * tm_size,)),
                dma((1,)),
            ],
            compiler_params=pltpu.CompilerParams(
                collective_id=0, has_side_effects=True, vmem_limit_bytes=60 * 2**20
            ),
        )(right_side, blocks, neighbors, shift_rates)
        block = pl.BlockSpec((2, steps, nodes), lambda e: (e, 0, 0))
        return pl.pallas_call(
            finish,
            grid=(plane // 2,),
            out_shape=jax.ShapeDtypeStruct(right_side.shape, f32),
            in_specs=[
                block,
                pl.BlockSpec((SWEEPS, half, nodes), lambda e: (0, 0, 0)),
                pl.BlockSpec((2, 2 * SWEEPS, nodes), lambda e: (e, 0, 0)),
            ],
            out_specs=block,
        )(series, table, start)

    return jax.shard_map(
        per_device,
        mesh=mesh,
        in_specs=(P("space", "tm", None), P("space", None, None, None), P("space", None), P()),
        out_specs=P("space", "tm", None),
        check_vma=False,
    )
```

```python
import functools

import jax
import jax.numpy as jnp
from jax import lax
from jax.experimental import pallas as pl
from jax.experimental.pallas import tpu as pltpu
from jax.sharding import PartitionSpec as P

SWEEPS = 4
SLOTS = 7
PIECES = (2, 2, 2, 1, 1)
CUTS = ((0, 4), (4, 3))
CHUNKS = len(PIECES)
ROWS = 8
WRAP_WEIGHT = 0.01
DIAG_WEIGHT = 6.0
BLOCK_WEIGHT = 3.0
STEP_SCALE = 0.1
MESH = pl.DeviceIdType.MESH


def split(value):
    hi = value.astype(jnp.bfloat16)
    lo = (value - hi.astype(jnp.float32)).astype(jnp.bfloat16)
    return hi, lo


def windows(half):
    unit = half // sum(PIECES)
    return [(unit * sum(PIECES[:c]), unit * PIECES[c]) for c in range(CHUNKS)]


def shares(plane):
    ends = (3 * plane) // 8
    rest = plane - ends
    kinds = []
    for lp in range(2):
        low = (rest + 1 - lp) // 2
        kinds.append([0] * ends + [1] * low + [2] * (rest - low))
    return kinds


def woven(kinds, lp):
    ends = [(lp, e) for e in range(len(kinds)) if kinds[e] == 0]
    low = [(lp, e) for e in range(len(kinds)) if kinds[e] == 1]
    high = [(lp, e) for e in range(len(kinds)) if kinds[e] == 2]
    middles = []
    while low or high:
        for side in (low, high) if lp == 0 else (high, low):
            if side:
                middles.append(side.pop(0))
    order = list(middles[: 2 - lp])
    for at, item in enumerate(ends):
        order.append(item)
        order += middles[2 - lp + at : 3 - lp + at]
    order += middles[2 - lp + len(ends) :]
    return middles, order


def kernel(
    tm_size, sp_size, x_ref, blocks_ref, near_ref, shift_ref,
    series_ref, table_ref, start_ref, *scratch
):
    plane, steps, nodes = x_ref.shape
    half = steps // 2
    spans = windows(half)
    moves = SWEEPS - 1
    groups = sp_size // 4
    segments = 2 * tm_size
    first_z = scratch[:CHUNKS]
    halos = scratch[CHUNKS : CHUNKS + 2 * moves * CHUNKS]
    (z1, z2, z3, series, held, weights, table, gathered, own, nearv, nears,
     w_recv, w_out, w_mate, w_fwd, d_recv, d_mate, d_out, n_recv, n_send, n_load,
     h_send, h_recv, r_send, r_recv, e_send, e_recv, t_store) = scratch[
        CHUNKS + 2 * moves * CHUNKS :
    ]
    zs = [None, z1, z2, z3]
    kinds = shares(plane)
    quad = tm_size % 4 == 0
    tm = lax.axis_index("tm")
    sp = lax.axis_index("space")
    group = sp // 4
    chip = (sp // 2) % 2
    core = sp % 2
    far_side = (chip + core) % 2
    far = far_side == 1
    near = far_side == 0
    layer = tm % 4 if quad else tm * 0
    middle = (layer == 1) | (layer == 2)
    end = (layer == 0) | (layer == 3)
    mate = group * 4 + chip * 2 + (1 - core)
    here_near = group * 4 + chip * 2 + chip
    there_far = group * 4 + (1 - chip) * 2 + chip
    across = ((group + groups + 2 * core - 1) % groups) * 4 + chip * 2 + (1 - core)

    def remote(src, dst, send, recv, **device):
        return pltpu.make_async_remote_copy(
            src_ref=src, dst_ref=dst, send_sem=send, recv_sem=recv,
            device_id=device, device_id_type=MESH,
        )

    def arrived(dst, recv):
        remote(dst, dst, n_send.at[0], recv, space=mate).wait_recv()

    barrier = pltpu.get_barrier_semaphore()
    greeted = 0
    for r in range(tm_size):
        for d in range(4):
            if r == 0 and d == 0:
                continue
            pl.semaphore_signal(
                barrier, inc=1, device_id_type=MESH,
                device_id={"tm": (tm + r) % tm_size, "space": group * 4 + (sp + d) % 4},
            )
            greeted += 1
    if groups > 1:
        pl.semaphore_signal(barrier, inc=1, device_id={"space": across}, device_id_type=MESH)
        greeted += 1

    def fetches(lp, e):
        if not quad or kinds[lp][e] == 0:
            return end
        return layer == kinds[lp][e]

    def piece(ref, *place):
        return ref.at[(*place[:-1], pl.ds(*CUTS[place[-1]]))]

    def own_load(e, q):
        return pltpu.make_async_copy(
            piece(blocks_ref, e, q), piece(held, 0, e, q), w_recv.at[0, e, q]
        )

    def own_data(k):
        first, width = spans[k]
        return pltpu.make_async_copy(
            x_ref.at[:, pl.ds(chip * half + first, width), :], first_z[k].at[0], d_recv.at[k, 0]
        )

    def mate_data(k):
        first, width = spans[k]
        return remote(
            x_ref.at[:, pl.ds(chip * half + first, width), :], first_z[k].at[1],
            d_mate.at[k], d_recv.at[k, 1], space=mate,
        )

    def out_data(k):
        first, width = spans[k]
        return remote(
            x_ref.at[:, pl.ds((1 - chip) * half + first, width), :], first_z[k].at[far_side],
            d_out.at[k], d_recv.at[k, far_side], space=there_far,
        )

    def out_blocks(lp, e, q):
        return remote(
            piece(blocks_ref, e, q) if lp == 0 else piece(held, 1, e, q), piece(held, lp, e, q),
            w_out.at[lp, e, q], w_recv.at[lp, e, q], space=there_far,
        )

    def mate_blocks(e, q):
        return remote(
            piece(blocks_ref, e, q), piece(held, 1, e, q), w_mate.at[e, q], w_recv.at[1, e, q],
            space=mate,
        )

    def out_near():
        return remote(
            near_ref, nearv.at[far_side], n_send.at[0], n_recv.at[far_side], space=there_far
        )

    def mate_near():
        return remote(near_ref, nearv.at[1], n_send.at[1], n_recv.at[1], space=mate)

    def forward(lp, e, q, up):
        return remote(
            piece(held, lp, e, q), piece(held, lp, e, q), w_fwd.at[lp, e, q, up],
            w_recv.at[lp, e, q], tm=tm + 1 if up else tm - 1,
        )

    def forwards(lp, e, q, act):
        if not quad:
            return
        downs, ups = (((3,), (0,)), ((1,), (1, 2)), ((2, 1), (2,)))[kinds[lp][e]]
        for way, layers in ((0, downs), (1, ups)):
            for at in layers:

                @pl.when(layer == at)
                def _():
                    act(forward(lp, e, q, way))

    def halo(j, k, d):
        return halos[(j * CHUNKS + k) * 2 + d]

    def part(j, k, lp):
        if j == 0:
            return first_z[k].at[lp]
        return zs[j].at[lp, :, pl.ds(*spans[k]), :]

    def transfer(j, k, d):
        return remote(
            part(j, k, d), halo(j, k, d), h_send.at[j, k, d], h_recv.at[j, k, d],
            space=across if d == 0 else mate,
        )

    @pl.when(near)
    def _():
        for e in range(plane):
            for q in range(len(CUTS)):
                own_load(e, q).start()
        for k in range(CHUNKS):
            own_data(k).start()
        pltpu.make_async_copy(near_ref, nearv.at[0], n_recv.at[0]).start()

    pl.semaphore_wait(barrier, greeted)

    out_near().start()

    @pl.when(end)
    def _():
        for k in range(CHUNKS):
            out_data(k).start()

    @pl.when(near)
    def _():
        for e in range(plane):

            @pl.when(fetches(0, e))
            def _():
                for q in range(len(CUTS)):
                    out_blocks(0, e, q).start()

    @pl.when(far)
    def _():
        mate_near().start()
        for k in range(CHUNKS):
            mate_data(k).start()
        for e in range(plane):
            for q in range(len(CUTS)):
                mate_blocks(e, q).start()

    sigmas = [STEP_SCALE * shift_ref[i] for i in range(SWEEPS)]
    rates = [1.0 / (1.0 + jnp.full((ROWS, nodes), sigma, jnp.float32)) for sigma in sigmas]

    def cascade(inputs, states):
        states = list(states)
        above = None
        for i in reversed(range(SWEEPS)):
            total = states[i] if inputs is None else inputs[i] + states[i]
            if above is not None:
                total = total + above
            states[i] = above = rates[i] * total
        return states

    row = lax.broadcasted_iota(jnp.int32, (ROWS, nodes), 0)
    unit = [(row == i).astype(jnp.float32) for i in range(SWEEPS)]

    def respond(g, states):
        kept = []
        for _ in range(ROWS):
            states = cascade(None, states)
            kept.append(states[0])
        flat = jnp.swapaxes(jnp.stack(kept), 0, 1)
        base = pl.multiple_of(g * ROWS, ROWS)
        for j in range(SWEEPS):
            table[j, pl.ds(base, ROWS), :] = flat[j]
        return tuple(states)

    over = lax.fori_loop(0, half // ROWS, respond, tuple(unit))
    save_table = pltpu.make_async_copy(table, table_ref, t_store.at[0])
    save_table.start()
    carry_of = [[over[i][j : j + 1, :] for j in range(SWEEPS)] for i in range(SWEEPS)]

    def advance(vectors):
        result = []
        for i in range(SWEEPS):
            total = carry_of[i][i] * vectors[i]
            for j in range(i + 1, SWEEPS):
                total = total + carry_of[i][j] * vectors[j]
            result.append(total)
        return result

    around = list(over)
    for _ in range(segments - 1):
        around = advance(around)

    def prepare(lp, e):
        outer_slot = 1 + (core if lp == 0 else 1 - core)
        for b in range(SLOTS):
            s = outer_slot if b == 1 else 3 - outer_slot if b == 2 else b
            hi, lo = split((-STEP_SCALE * BLOCK_WEIGHT) * held[lp, e, s].T)
            weights[lp, e, b * nodes : (b + 1) * nodes, :nodes] = hi
            weights[lp, e, b * nodes : (b + 1) * nodes, nodes:] = lo

    def prepare_all(lp):
        def one(e, _):
            prepare(lp, e)
            return 0

        lax.fori_loop(0, plane, one, 0)

    @pl.when(near)
    def _():
        for e in range(plane):
            for q in range(len(CUTS)):
                arrived(piece(held, 1, e, q), w_recv.at[1, e, q])

                @pl.when(fetches(1, e))
                def _():
                    out_blocks(1, e, q).start()

        @pl.when(middle)
        def _():
            for k in range(CHUNKS):
                out_data(k).start()

        for k in range(CHUNKS):
            for lp in range(2):
                arrived(first_z[k].at[lp], d_recv.at[k, lp])
                transfer(0, k, lp).start()
        for e in range(plane):
            for q in range(len(CUTS)):
                own_load(e, q).wait()
        prepare_all(0)
        prepare_all(1)

    def take(lp, e):
        for q in range(len(CUTS)):
            arrived(piece(held, lp, e, q), w_recv.at[lp, e, q])
            forwards(lp, e, q, lambda copy: copy.start())

    between = [woven(kinds[lp], lp) for lp in range(2)]
    ends = sum(kind == 0 for kind in kinds[0])
    for side in (1, 2):

        @pl.when(far & (layer == side))
        def _():
            mine = [(lp, e) for lp in range(2) for e in range(plane) if kinds[lp][e] == side]
            theirs = [(lp, e) for lp in range(2) for e in range(plane) if kinds[lp][e] == 3 - side]
            for i in range(max(len(mine), len(theirs) + 2)):
                if i < len(mine):
                    take(*mine[i])
                if i == len(mine) - 1:
                    for k in range(CHUNKS):
                        out_data(k).start()
                if 0 <= i - 1 < len(theirs):
                    take(*theirs[i - 1])

    @pl.when(far & middle)
    def _():
        for lp in range(2):

            def one(e, _):
                prepare(lp, e)
                return 0

            lax.fori_loop(ends, plane, one, 0)

    @pl.when(far)
    def _():
        for k in range(CHUNKS):
            for lp in range(2):
                arrived(first_z[k].at[lp], d_recv.at[k, lp])
                transfer(0, k, lp).start()

    def receive_all(lp):
        for _, e in between[lp][1]:

            @pl.when(far & (end if kinds[lp][e] else layer >= 0))
            def _():
                take(lp, e)
                prepare(lp, e)

    receive_all(0)

    for lp in range(2):
        arrived(nearv.at[lp], n_recv.at[lp])
    load_near = pltpu.make_async_copy(nearv, nears, n_load.at[0])
    load_near.start()
    load_near.wait()

    def apply(j, k, lp):
        first, width = spans[k]
        window = pl.ds(first, width)
        diag = sigmas[j] - STEP_SCALE * DIAG_WEIGHT
        outer_slot = 1 + (core if lp == 0 else 1 - core)

        def source(q, index):
            return first_z[k][q, index] if j == 0 else zs[j][q, index, window, :]

        def one(e, _):
            def near_of(s):
                return lax.rem(nears[lp, e, s], plane)

            here = source(lp, e)
            parts = [
                here,
                halo(j, k, lp)[near_of(outer_slot)],
                source(1 - lp, near_of(3 - outer_slot)),
            ] + [source(lp, near_of(s)) for s in range(3, SLOTS)]
            pairs = [split(p) for p in parts]
            hi = jnp.concatenate([p[0] for p in pairs], axis=1)
            lo = jnp.concatenate([p[1] for p in pairs], axis=1)
            rows = jnp.concatenate([hi, lo], axis=0)
            both = jnp.dot(rows, weights[lp, e], preferred_element_type=jnp.float32)
            both = both[:width] + both[width:]
            zs[j + 1][lp, e, window, :] = diag * here + both[:, :nodes] + both[:, nodes:]
            return 0

        lax.fori_loop(0, plane, one, 0, unroll=4)

    def move(j, k, lp):
        transfer(j, k, lp).wait_recv()
        apply(j, k, lp)
        if j + 1 < moves:
            transfer(j + 1, k, lp).start()

    for k in range(CHUNKS):
        move(0, k, 0)
    receive_all(1)

    def back_target(lp):
        return group * 4 + 2 * core + (core + lp) % 2

    def give_back(k, lp):
        first, width = spans[k]
        return remote(
            series.at[lp, :, pl.ds(first, width), :],
            series_ref.at[:, pl.ds(chip * half + first, width), :],
            r_send.at[k, lp], r_recv.at[k, chip], space=back_target(lp),
        )

    def keep_back(k):
        first, width = spans[k]
        return pltpu.make_async_copy(
            series.at[0, :, pl.ds(first, width), :],
            series_ref.at[:, pl.ds(chip * half + first, width), :],
            r_recv.at[k, chip],
        )

    states = tuple(jnp.zeros((ROWS, nodes), jnp.float32) for _ in range(2 * SWEEPS))
    def conclude(k, states):
        first, width = spans[k]
        for lp in range(2):
            move(2, k, lp)

        def scan(g, states):
            states = list(states)
            base = pl.multiple_of(first + g * ROWS, ROWS)
            inner = pl.multiple_of(g * ROWS, ROWS)
            for lp in range(2):
                mine = states[lp * SWEEPS : (lp + 1) * SWEEPS]
                here = [jnp.swapaxes(first_z[k][lp, :, pl.ds(inner, ROWS), :], 0, 1)] + [
                    jnp.swapaxes(z[lp, :, pl.ds(base, ROWS), :], 0, 1) for z in zs[1:]
                ]
                kept = []
                for t in range(ROWS):
                    mine = cascade([h[t] for h in here], mine)
                    kept.append(mine[0])
                series[lp, :, pl.ds(base, ROWS), :] = jnp.swapaxes(jnp.stack(kept), 0, 1)
                states[lp * SWEEPS : (lp + 1) * SWEEPS] = mine
            return tuple(states)

        states = lax.fori_loop(0, width // ROWS, scan, states)
        give_back(k, 1).start()

        @pl.when(far)
        def _():
            give_back(k, 0).start()

        @pl.when(near)
        def _():
            keep_back(k).start()

        return states

    for k in range(CHUNKS + 2):
        if k < CHUNKS:
            move(0, k, 1)
            move(1, k, 0)
        if 0 <= k - 1 < CHUNKS:
            move(1, k - 1, 1)
        if k >= 2:
            states = conclude(k - 2, states)

    for lp in range(2):
        for i in range(SWEEPS):
            own[lp, i] = states[lp * SWEEPS + i]
    segment = 2 * tm + chip

    def give_end(r, lp):
        return remote(
            own.at[lp], gathered.at[segment], e_send.at[r, lp], e_recv.at[segment],
            tm=(tm + r) % tm_size, space=back_target(lp),
        )

    for r in range(tm_size):
        for lp in range(2):
            if r == 0 and lp == 0:

                @pl.when(far)
                def _():
                    give_end(0, 0).start()

                @pl.when(near)
                def _():
                    pltpu.make_async_copy(
                        own.at[0], gathered.at[segment], e_recv.at[segment]
                    ).start()
            else:
                give_end(r, lp).start()
    for s in range(segments):
        arrived(gathered.at[s], e_recv.at[s])

    def ends(back):
        return [gathered[(2 * tm + segments - back) % segments, i] for i in range(SWEEPS)]

    def enter(back):
        entered = (2 * tm - back + 1 + segments) % segments
        return jnp.where(entered == 0, jnp.float32(WRAP_WEIGHT), jnp.float32(1.0))

    total = [enter(segments) * value for value in ends(segments)]
    for back in range(segments - 1, 0, -1):
        moved = advance(total)
        total = [enter(back) * (a + b) for a, b in zip(ends(back), moved)]
    start = [None] * SWEEPS
    for i in reversed(range(SWEEPS)):
        value = total[i]
        for j in range(i + 1, SWEEPS):
            value = value + WRAP_WEIGHT * around[i][j : j + 1, :] * start[j]
        start[i] = value / (1.0 - WRAP_WEIGHT * around[i][i : i + 1, :])
    later = [a + b for a, b in zip(ends(segments), advance(start))]
    for e in range(plane):
        for i in range(SWEEPS):
            start_ref[e, i : i + 1, :] = start[i][e : e + 1, :]
            start_ref[e, SWEEPS + i : SWEEPS + i + 1, :] = later[i][e : e + 1, :]

    save_table.wait()
    for k in range(CHUNKS):
        first, width = spans[k]
        for h in range(2):
            arrived(series_ref.at[:, pl.ds(h * half + first, width), :], r_recv.at[k, h])
    out_near().wait_send()
    for k in range(CHUNKS):
        out_data(k).wait_send()
        give_back(k, 1).wait_send()
        for j in range(moves):
            for d in range(2):
                transfer(j, k, d).wait_send()
    for r in range(tm_size):
        for lp in range(2):
            if r or lp:
                give_end(r, lp).wait_send()

    @pl.when(near)
    def _():
        for e in range(plane):
            for lp in range(2):

                @pl.when(fetches(lp, e))
                def _():
                    for q in range(len(CUTS)):
                        out_blocks(lp, e, q).wait_send()

    @pl.when(far)
    def _():
        mate_near().wait_send()
        give_end(0, 0).wait_send()
        for k in range(CHUNKS):
            mate_data(k).wait_send()
            give_back(k, 0).wait_send()
        for e in range(plane):
            for q in range(len(CUTS)):
                mate_blocks(e, q).wait_send()
                for lp in range(2):
                    forwards(lp, e, q, lambda copy: copy.wait_send())


def finish(series_ref, table_ref, start_ref, out_ref):
    half = series_ref.shape[1] // 2

    def some(g, _):
        rows = pl.ds(pl.multiple_of(g * 4 * ROWS, 4 * ROWS), 4 * ROWS)
        lines = [table_ref[i, rows, :] for i in range(SWEEPS)]
        for h in range(2):
            place = pl.ds(pl.multiple_of(h * half + g * 4 * ROWS, 4 * ROWS), 4 * ROWS)
            for e in range(series_ref.shape[0]):
                value = series_ref[e, place, :]
                for i in range(SWEEPS):
                    row = h * SWEEPS + i
                    value = value + lines[i] * start_ref[e, row : row + 1, :]
                out_ref[e, place, :] = value
        return 0

    lax.fori_loop(0, half // (4 * ROWS), some, 0)


def solution(mesh):
    tm_size, sp_size = mesh.shape["tm"], mesh.shape["space"]

    def per_device(right_side, blocks, neighbors, shift_rates):
        plane, steps, nodes = right_side.shape
        half = steps // 2
        moves = SWEEPS - 1
        f32 = jnp.float32
        dma = pltpu.SemaphoreType.DMA
        whole = pltpu.VMEM((2, plane, half, nodes), f32)
        widths = [width for _, width in windows(half)]
        series, table, start = pl.pallas_call(
            functools.partial(kernel, tm_size, sp_size),
            out_shape=(
                jax.ShapeDtypeStruct(right_side.shape, f32),
                jax.ShapeDtypeStruct((SWEEPS, half, nodes), f32),
                jax.ShapeDtypeStruct((plane, 2 * SWEEPS, nodes), f32),
            ),
            in_specs=[
                pl.BlockSpec(memory_space=pl.ANY),
                pl.BlockSpec(memory_space=pl.ANY),
                pl.BlockSpec(memory_space=pl.ANY),
                pl.BlockSpec(memory_space=pltpu.SMEM),
            ],
            out_specs=(
                pl.BlockSpec(memory_space=pl.ANY),
                pl.BlockSpec(memory_space=pl.ANY),
                pl.BlockSpec(memory_space=pltpu.VMEM),
            ),
            scratch_shapes=[pltpu.VMEM((2, plane, width, nodes), f32) for width in widths]
            + [
                pltpu.VMEM((plane, width, nodes), f32)
                for _ in range(moves) for width in widths for _ in range(2)
            ]
            + [
                whole, whole, whole, whole,
                pltpu.VMEM((2,) + blocks.shape, f32),
                pltpu.VMEM((2, plane, SLOTS * nodes, 2 * nodes), jnp.bfloat16),
                pltpu.VMEM((SWEEPS, half, nodes), f32),
                pltpu.VMEM((2 * tm_size, SWEEPS, plane, nodes), f32),
                pltpu.VMEM((2, SWEEPS, plane, nodes), f32),
                pltpu.VMEM((2,) + neighbors.shape, jnp.int32),
                pltpu.SMEM((2,) + neighbors.shape, jnp.int32),
                dma((2, plane, len(CUTS))),
                dma((2, plane, len(CUTS))),
                dma((plane, len(CUTS))),
                dma((2, plane, len(CUTS), 2)),
                dma((CHUNKS, 2)),
                dma((CHUNKS,)),
                dma((CHUNKS,)),
                dma((2,)),
                dma((2,)),
                dma((1,)),
                dma((moves, CHUNKS, 2)),
                dma((moves, CHUNKS, 2)),
                dma((CHUNKS, 2)),
                dma((CHUNKS, 2)),
                dma((tm_size, 2)),
                dma((2 * tm_size,)),
                dma((1,)),
            ],
            compiler_params=pltpu.CompilerParams(
                collective_id=0, has_side_effects=True, vmem_limit_bytes=60 * 2**20
            ),
        )(right_side, blocks, neighbors, shift_rates)
        block = pl.BlockSpec((2, steps, nodes), lambda e: (e, 0, 0))
        return pl.pallas_call(
            finish,
            grid=(plane // 2,),
            out_shape=jax.ShapeDtypeStruct(right_side.shape, f32),
            in_specs=[
                block,
                pl.BlockSpec((SWEEPS, half, nodes), lambda e: (0, 0, 0)),
                pl.BlockSpec((2, 2 * SWEEPS, nodes), lambda e: (e, 0, 0)),
            ],
            out_specs=block,
        )(series, table, start)

    return jax.shard_map(
        per_device,
        mesh=mesh,
        in_specs=(P("space", "tm", None), P("space", None, None, None), P("space", None), P()),
        out_specs=P("space", "tm", None),
        check_vma=False,
    )
```

```python
import functools

import jax
import jax.numpy as jnp
from jax import lax
from jax.experimental import pallas as pl
from jax.experimental.pallas import tpu as pltpu
from jax.sharding import PartitionSpec as P

SWEEPS = 4
SLOTS = 7
PIECES = (2, 2, 2, 1, 1)
CUTS = ((0, 4), (4, 3))
CHUNKS = len(PIECES)
ROWS = 8
WRAP_WEIGHT = 0.01
DIAG_WEIGHT = 6.0
BLOCK_WEIGHT = 3.0
STEP_SCALE = 0.1
MESH = pl.DeviceIdType.MESH


def split(value):
    hi = value.astype(jnp.bfloat16)
    lo = (value - hi.astype(jnp.float32)).astype(jnp.bfloat16)
    return hi, lo


def windows(half):
    unit = half // sum(PIECES)
    return [(unit * sum(PIECES[:c]), unit * PIECES[c]) for c in range(CHUNKS)]


def shares(plane):
    kinds = []
    for lp in range(2):
        ends = (7 * plane + 8 * (1 - lp)) // 16
        rest = plane - ends
        low = (rest + 1 - lp) // 2
        kinds.append([0] * ends + [1] * low + [2] * (rest - low))
    return kinds


def woven(kinds, lp):
    ends = [(lp, e) for e in range(len(kinds)) if kinds[e] == 0]
    low = [(lp, e) for e in range(len(kinds)) if kinds[e] == 1]
    high = [(lp, e) for e in range(len(kinds)) if kinds[e] == 2]
    middles = []
    while low or high:
        for side in (low, high) if lp == 0 else (high, low):
            if side:
                middles.append(side.pop(0))
    order = list(middles[: 2 - lp])
    for at, item in enumerate(ends):
        order.append(item)
        order += middles[2 - lp + at : 3 - lp + at]
    order += middles[2 - lp + len(ends) :]
    return middles, order


def kernel(
    tm_size, sp_size, x_ref, blocks_ref, near_ref, shift_ref,
    series_ref, table_ref, start_ref, *scratch
):
    plane, steps, nodes = x_ref.shape
    half = steps // 2
    spans = windows(half)
    moves = SWEEPS - 1
    groups = sp_size // 4
    segments = 2 * tm_size
    first_z = scratch[:CHUNKS]
    halos = scratch[CHUNKS : CHUNKS + 2 * moves * CHUNKS]
    (z1, z2, z3, series, held, weights, table, gathered, own, nearv, nears,
     w_recv, w_out, w_mate, w_fwd, d_recv, d_mate, d_out, n_recv, n_send, n_load,
     h_send, h_recv, r_send, r_recv, e_send, e_recv, t_store) = scratch[
        CHUNKS + 2 * moves * CHUNKS :
    ]
    zs = [None, z1, z2, z3]
    kinds = shares(plane)
    quad = tm_size % 4 == 0
    tm = lax.axis_index("tm")
    sp = lax.axis_index("space")
    group = sp // 4
    chip = (sp // 2) % 2
    core = sp % 2
    far_side = (chip + core) % 2
    far = far_side == 1
    near = far_side == 0
    layer = tm % 4 if quad else tm * 0
    middle = (layer == 1) | (layer == 2)
    end = (layer == 0) | (layer == 3)
    mate = group * 4 + chip * 2 + (1 - core)
    here_near = group * 4 + chip * 2 + chip
    there_far = group * 4 + (1 - chip) * 2 + chip
    across = ((group + groups + 2 * core - 1) % groups) * 4 + chip * 2 + (1 - core)

    def remote(src, dst, send, recv, **device):
        return pltpu.make_async_remote_copy(
            src_ref=src, dst_ref=dst, send_sem=send, recv_sem=recv,
            device_id=device, device_id_type=MESH,
        )

    def arrived(dst, recv):
        remote(dst, dst, n_send.at[0], recv, space=mate).wait_recv()

    barrier = pltpu.get_barrier_semaphore()
    greeted = 0
    for r in range(tm_size):
        for d in range(4):
            if r == 0 and d == 0:
                continue
            pl.semaphore_signal(
                barrier, inc=1, device_id_type=MESH,
                device_id={"tm": (tm + r) % tm_size, "space": group * 4 + (sp + d) % 4},
            )
            greeted += 1
    if groups > 1:
        pl.semaphore_signal(barrier, inc=1, device_id={"space": across}, device_id_type=MESH)
        greeted += 1

    def fetches(lp, e):
        if not quad or kinds[lp][e] == 0:
            return end
        return layer == kinds[lp][e]

    def piece(ref, *place):
        return ref.at[(*place[:-1], pl.ds(*CUTS[place[-1]]))]

    def own_load(e, q):
        return pltpu.make_async_copy(
            piece(blocks_ref, e, q), piece(held, 0, e, q), w_recv.at[0, e, q]
        )

    def own_data(k):
        first, width = spans[k]
        return pltpu.make_async_copy(
            x_ref.at[:, pl.ds(chip * half + first, width), :], first_z[k].at[0], d_recv.at[k, 0]
        )

    def mate_data(k):
        first, width = spans[k]
        return remote(
            x_ref.at[:, pl.ds(chip * half + first, width), :], first_z[k].at[1],
            d_mate.at[k], d_recv.at[k, 1], space=mate,
        )

    def out_data(k):
        first, width = spans[k]
        return remote(
            x_ref.at[:, pl.ds((1 - chip) * half + first, width), :], first_z[k].at[far_side],
            d_out.at[k], d_recv.at[k, far_side], space=there_far,
        )

    def out_blocks(lp, e, q):
        return remote(
            piece(blocks_ref, e, q) if lp == 0 else piece(held, 1, e, q), piece(held, lp, e, q),
            w_out.at[lp, e, q], w_recv.at[lp, e, q], space=there_far,
        )

    def mate_blocks(e, q):
        return remote(
            piece(blocks_ref, e, q), piece(held, 1, e, q), w_mate.at[e, q], w_recv.at[1, e, q],
            space=mate,
        )

    def out_near():
        return remote(
            near_ref, nearv.at[far_side], n_send.at[0], n_recv.at[far_side], space=there_far
        )

    def mate_near():
        return remote(near_ref, nearv.at[1], n_send.at[1], n_recv.at[1], space=mate)

    def forward(lp, e, q, up):
        return remote(
            piece(held, lp, e, q), piece(held, lp, e, q), w_fwd.at[lp, e, q, up],
            w_recv.at[lp, e, q], tm=tm + 1 if up else tm - 1,
        )

    def forwards(lp, e, q, act):
        if not quad:
            return
        downs, ups = (((3,), (0,)), ((1,), (1, 2)), ((2, 1), (2,)))[kinds[lp][e]]
        for way, layers in ((0, downs), (1, ups)):
            for at in layers:

                @pl.when(layer == at)
                def _():
                    act(forward(lp, e, q, way))

    def halo(j, k, d):
        return halos[(j * CHUNKS + k) * 2 + d]

    def part(j, k, lp):
        if j == 0:
            return first_z[k].at[lp]
        return zs[j].at[lp, :, pl.ds(*spans[k]), :]

    def transfer(j, k, d):
        return remote(
            part(j, k, d), halo(j, k, d), h_send.at[j, k, d], h_recv.at[j, k, d],
            space=across if d == 0 else mate,
        )

    @pl.when(near)
    def _():
        for e in range(plane):
            for q in range(len(CUTS)):
                own_load(e, q).start()
        for k in range(CHUNKS):
            own_data(k).start()
        pltpu.make_async_copy(near_ref, nearv.at[0], n_recv.at[0]).start()

    pl.semaphore_wait(barrier, greeted)

    out_near().start()

    @pl.when(end)
    def _():
        for k in range(CHUNKS):
            out_data(k).start()

    @pl.when(near)
    def _():
        for e in range(plane):

            @pl.when(fetches(0, e))
            def _():
                for q in range(len(CUTS)):
                    out_blocks(0, e, q).start()

    @pl.when(far)
    def _():
        mate_near().start()
        for k in range(CHUNKS):
            mate_data(k).start()
        for e in range(plane):
            for q in range(len(CUTS)):
                mate_blocks(e, q).start()

    sigmas = [STEP_SCALE * shift_ref[i] for i in range(SWEEPS)]
    rates = [1.0 / (1.0 + jnp.full((ROWS, nodes), sigma, jnp.float32)) for sigma in sigmas]

    def cascade(inputs, states):
        states = list(states)
        above = None
        for i in reversed(range(SWEEPS)):
            total = states[i] if inputs is None else inputs[i] + states[i]
            if above is not None:
                total = total + above
            states[i] = above = rates[i] * total
        return states

    row = lax.broadcasted_iota(jnp.int32, (ROWS, nodes), 0)
    unit = [(row == i).astype(jnp.float32) for i in range(SWEEPS)]

    def respond(g, states):
        kept = []
        for _ in range(ROWS):
            states = cascade(None, states)
            kept.append(states[0])
        flat = jnp.swapaxes(jnp.stack(kept), 0, 1)
        base = pl.multiple_of(g * ROWS, ROWS)
        for j in range(SWEEPS):
            table[j, pl.ds(base, ROWS), :] = flat[j]
        return tuple(states)

    over = lax.fori_loop(0, half // ROWS, respond, tuple(unit))
    save_table = pltpu.make_async_copy(table, table_ref, t_store.at[0])
    save_table.start()
    carry_of = [[over[i][j : j + 1, :] for j in range(SWEEPS)] for i in range(SWEEPS)]

    def advance(vectors):
        result = []
        for i in range(SWEEPS):
            total = carry_of[i][i] * vectors[i]
            for j in range(i + 1, SWEEPS):
                total = total + carry_of[i][j] * vectors[j]
            result.append(total)
        return result

    around = list(over)
    for _ in range(segments - 1):
        around = advance(around)

    def prepare(lp, e):
        outer_slot = 1 + (core if lp == 0 else 1 - core)
        for b in range(SLOTS):
            s = outer_slot if b == 1 else 3 - outer_slot if b == 2 else b
            hi, lo = split((-STEP_SCALE * BLOCK_WEIGHT) * held[lp, e, s].T)
            weights[lp, e, b * nodes : (b + 1) * nodes, :nodes] = hi
            weights[lp, e, b * nodes : (b + 1) * nodes, nodes:] = lo

    def prepare_all(lp):
        def one(e, _):
            prepare(lp, e)
            return 0

        lax.fori_loop(0, plane, one, 0)

    @pl.when(near)
    def _():
        for e in range(plane):
            for q in range(len(CUTS)):
                arrived(piece(held, 1, e, q), w_recv.at[1, e, q])

                @pl.when(fetches(1, e))
                def _():
                    out_blocks(1, e, q).start()

        @pl.when(middle)
        def _():
            for k in range(CHUNKS):
                out_data(k).start()

        for k in range(CHUNKS):
            for lp in range(2):
                arrived(first_z[k].at[lp], d_recv.at[k, lp])
                transfer(0, k, lp).start()
        for e in range(plane):
            for q in range(len(CUTS)):
                own_load(e, q).wait()
        prepare_all(0)
        prepare_all(1)

    def take(lp, e):
        for q in range(len(CUTS)):
            arrived(piece(held, lp, e, q), w_recv.at[lp, e, q])
            forwards(lp, e, q, lambda copy: copy.start())

    between = [woven(kinds[lp], lp) for lp in range(2)]
    for side in (1, 2):

        @pl.when(far & (layer == side))
        def _():
            mine = [(lp, e) for lp in range(2) for e in range(plane) if kinds[lp][e] == side]
            theirs = [(lp, e) for lp in range(2) for e in range(plane) if kinds[lp][e] == 3 - side]
            for i in range(max(len(mine), len(theirs) + 2)):
                if i < len(mine):
                    take(*mine[i])
                if i == len(mine) - 1:
                    for k in range(CHUNKS):
                        out_data(k).start()
                if 0 <= i - 1 < len(theirs):
                    take(*theirs[i - 1])

    @pl.when(far & middle)
    def _():
        for lp in range(2):

            def one(e, _):
                prepare(lp, e)
                return 0

            lax.fori_loop(sum(kind == 0 for kind in kinds[lp]), plane, one, 0)

    @pl.when(far)
    def _():
        for k in range(CHUNKS):
            for lp in range(2):
                arrived(first_z[k].at[lp], d_recv.at[k, lp])
                transfer(0, k, lp).start()

    def receive_all(lp):
        for _, e in between[lp][1]:

            @pl.when(far & (end if kinds[lp][e] else layer >= 0))
            def _():
                take(lp, e)
                prepare(lp, e)

    receive_all(0)

    for lp in range(2):
        arrived(nearv.at[lp], n_recv.at[lp])
    load_near = pltpu.make_async_copy(nearv, nears, n_load.at[0])
    load_near.start()
    load_near.wait()

    def apply(j, k, lp):
        first, width = spans[k]
        window = pl.ds(first, width)
        diag = sigmas[j] - STEP_SCALE * DIAG_WEIGHT
        outer_slot = 1 + (core if lp == 0 else 1 - core)

        def source(q, index):
            return first_z[k][q, index] if j == 0 else zs[j][q, index, window, :]

        def one(e, _):
            def near_of(s):
                return lax.rem(nears[lp, e, s], plane)

            here = source(lp, e)
            parts = [
                here,
                halo(j, k, lp)[near_of(outer_slot)],
                source(1 - lp, near_of(3 - outer_slot)),
            ] + [source(lp, near_of(s)) for s in range(3, SLOTS)]
            pairs = [split(p) for p in parts]
            hi = jnp.concatenate([p[0] for p in pairs], axis=1)
            lo = jnp.concatenate([p[1] for p in pairs], axis=1)
            rows = jnp.concatenate([hi, lo], axis=0)
            both = jnp.dot(rows, weights[lp, e], preferred_element_type=jnp.float32)
            both = both[:width] + both[width:]
            zs[j + 1][lp, e, window, :] = diag * here + both[:, :nodes] + both[:, nodes:]
            return 0

        lax.fori_loop(0, plane, one, 0, unroll=4)

    def move(j, k, lp):
        transfer(j, k, lp).wait_recv()
        apply(j, k, lp)
        if j + 1 < moves:
            transfer(j + 1, k, lp).start()

    for k in range(CHUNKS):
        move(0, k, 0)
    receive_all(1)

    def back_target(lp):
        return group * 4 + 2 * core + (core + lp) % 2

    def give_back(k, lp):
        first, width = spans[k]
        return remote(
            series.at[lp, :, pl.ds(first, width), :],
            series_ref.at[:, pl.ds(chip * half + first, width), :],
            r_send.at[k, lp], r_recv.at[k, chip], space=back_target(lp),
        )

    def keep_back(k):
        first, width = spans[k]
        return pltpu.make_async_copy(
            series.at[0, :, pl.ds(first, width), :],
            series_ref.at[:, pl.ds(chip * half + first, width), :],
            r_recv.at[k, chip],
        )

    states = tuple(jnp.zeros((ROWS, nodes), jnp.float32) for _ in range(2 * SWEEPS))
    def conclude(k, states):
        first, width = spans[k]
        for lp in range(2):
            move(2, k, lp)

        def scan(g, states):
            states = list(states)
            base = pl.multiple_of(first + g * ROWS, ROWS)
            inner = pl.multiple_of(g * ROWS, ROWS)
            for lp in range(2):
                mine = states[lp * SWEEPS : (lp + 1) * SWEEPS]
                here = [jnp.swapaxes(first_z[k][lp, :, pl.ds(inner, ROWS), :], 0, 1)] + [
                    jnp.swapaxes(z[lp, :, pl.ds(base, ROWS), :], 0, 1) for z in zs[1:]
                ]
                kept = []
                for t in range(ROWS):
                    mine = cascade([h[t] for h in here], mine)
                    kept.append(mine[0])
                series[lp, :, pl.ds(base, ROWS), :] = jnp.swapaxes(jnp.stack(kept), 0, 1)
                states[lp * SWEEPS : (lp + 1) * SWEEPS] = mine
            return tuple(states)

        states = lax.fori_loop(0, width // ROWS, scan, states)
        give_back(k, 1).start()

        @pl.when(far)
        def _():
            give_back(k, 0).start()

        @pl.when(near)
        def _():
            keep_back(k).start()

        return states

    for k in range(CHUNKS + 2):
        if k < CHUNKS:
            move(0, k, 1)
            move(1, k, 0)
        if 0 <= k - 1 < CHUNKS:
            move(1, k - 1, 1)
        if k >= 2:
            states = conclude(k - 2, states)

    for lp in range(2):
        for i in range(SWEEPS):
            own[lp, i] = states[lp * SWEEPS + i]
    segment = 2 * tm + chip

    def give_end(r, lp):
        return remote(
            own.at[lp], gathered.at[segment], e_send.at[r, lp], e_recv.at[segment],
            tm=(tm + r) % tm_size, space=back_target(lp),
        )

    for r in range(tm_size):
        for lp in range(2):
            if r == 0 and lp == 0:

                @pl.when(far)
                def _():
                    give_end(0, 0).start()

                @pl.when(near)
                def _():
                    pltpu.make_async_copy(
                        own.at[0], gathered.at[segment], e_recv.at[segment]
                    ).start()
            else:
                give_end(r, lp).start()
    for s in range(segments):
        arrived(gathered.at[s], e_recv.at[s])

    def ends(back):
        return [gathered[(2 * tm + segments - back) % segments, i] for i in range(SWEEPS)]

    def enter(back):
        entered = (2 * tm - back + 1 + segments) % segments
        return jnp.where(entered == 0, jnp.float32(WRAP_WEIGHT), jnp.float32(1.0))

    total = [enter(segments) * value for value in ends(segments)]
    for back in range(segments - 1, 0, -1):
        moved = advance(total)
        total = [enter(back) * (a + b) for a, b in zip(ends(back), moved)]
    start = [None] * SWEEPS
    for i in reversed(range(SWEEPS)):
        value = total[i]
        for j in range(i + 1, SWEEPS):
            value = value + WRAP_WEIGHT * around[i][j : j + 1, :] * start[j]
        start[i] = value / (1.0 - WRAP_WEIGHT * around[i][i : i + 1, :])
    later = [a + b for a, b in zip(ends(segments), advance(start))]
    for e in range(plane):
        for i in range(SWEEPS):
            start_ref[e, i : i + 1, :] = start[i][e : e + 1, :]
            start_ref[e, SWEEPS + i : SWEEPS + i + 1, :] = later[i][e : e + 1, :]

    save_table.wait()
    for k in range(CHUNKS):
        first, width = spans[k]
        for h in range(2):
            arrived(series_ref.at[:, pl.ds(h * half + first, width), :], r_recv.at[k, h])
    out_near().wait_send()
    for k in range(CHUNKS):
        out_data(k).wait_send()
        give_back(k, 1).wait_send()
        for j in range(moves):
            for d in range(2):
                transfer(j, k, d).wait_send()
    for r in range(tm_size):
        for lp in range(2):
            if r or lp:
                give_end(r, lp).wait_send()

    @pl.when(near)
    def _():
        for e in range(plane):
            for lp in range(2):

                @pl.when(fetches(lp, e))
                def _():
                    for q in range(len(CUTS)):
                        out_blocks(lp, e, q).wait_send()

    @pl.when(far)
    def _():
        mate_near().wait_send()
        give_end(0, 0).wait_send()
        for k in range(CHUNKS):
            mate_data(k).wait_send()
            give_back(k, 0).wait_send()
        for e in range(plane):
            for q in range(len(CUTS)):
                mate_blocks(e, q).wait_send()
                for lp in range(2):
                    forwards(lp, e, q, lambda copy: copy.wait_send())


def finish(series_ref, table_ref, start_ref, out_ref):
    half = series_ref.shape[1] // 2

    def some(g, _):
        rows = pl.ds(pl.multiple_of(g * 4 * ROWS, 4 * ROWS), 4 * ROWS)
        lines = [table_ref[i, rows, :] for i in range(SWEEPS)]
        for h in range(2):
            place = pl.ds(pl.multiple_of(h * half + g * 4 * ROWS, 4 * ROWS), 4 * ROWS)
            for e in range(series_ref.shape[0]):
                value = series_ref[e, place, :]
                for i in range(SWEEPS):
                    row = h * SWEEPS + i
                    value = value + lines[i] * start_ref[e, row : row + 1, :]
                out_ref[e, place, :] = value
        return 0

    lax.fori_loop(0, half // (4 * ROWS), some, 0)


def solution(mesh):
    tm_size, sp_size = mesh.shape["tm"], mesh.shape["space"]

    def per_device(right_side, blocks, neighbors, shift_rates):
        plane, steps, nodes = right_side.shape
        half = steps // 2
        moves = SWEEPS - 1
        f32 = jnp.float32
        dma = pltpu.SemaphoreType.DMA
        whole = pltpu.VMEM((2, plane, half, nodes), f32)
        widths = [width for _, width in windows(half)]
        series, table, start = pl.pallas_call(
            functools.partial(kernel, tm_size, sp_size),
            out_shape=(
                jax.ShapeDtypeStruct(right_side.shape, f32),
                jax.ShapeDtypeStruct((SWEEPS, half, nodes), f32),
                jax.ShapeDtypeStruct((plane, 2 * SWEEPS, nodes), f32),
            ),
            in_specs=[
                pl.BlockSpec(memory_space=pl.ANY),
                pl.BlockSpec(memory_space=pl.ANY),
                pl.BlockSpec(memory_space=pl.ANY),
                pl.BlockSpec(memory_space=pltpu.SMEM),
            ],
            out_specs=(
                pl.BlockSpec(memory_space=pl.ANY),
                pl.BlockSpec(memory_space=pl.ANY),
                pl.BlockSpec(memory_space=pltpu.VMEM),
            ),
            scratch_shapes=[pltpu.VMEM((2, plane, width, nodes), f32) for width in widths]
            + [
                pltpu.VMEM((plane, width, nodes), f32)
                for _ in range(moves) for width in widths for _ in range(2)
            ]
            + [
                whole, whole, whole, whole,
                pltpu.VMEM((2,) + blocks.shape, f32),
                pltpu.VMEM((2, plane, SLOTS * nodes, 2 * nodes), jnp.bfloat16),
                pltpu.VMEM((SWEEPS, half, nodes), f32),
                pltpu.VMEM((2 * tm_size, SWEEPS, plane, nodes), f32),
                pltpu.VMEM((2, SWEEPS, plane, nodes), f32),
                pltpu.VMEM((2,) + neighbors.shape, jnp.int32),
                pltpu.SMEM((2,) + neighbors.shape, jnp.int32),
                dma((2, plane, len(CUTS))),
                dma((2, plane, len(CUTS))),
                dma((plane, len(CUTS))),
                dma((2, plane, len(CUTS), 2)),
                dma((CHUNKS, 2)),
                dma((CHUNKS,)),
                dma((CHUNKS,)),
                dma((2,)),
                dma((2,)),
                dma((1,)),
                dma((moves, CHUNKS, 2)),
                dma((moves, CHUNKS, 2)),
                dma((CHUNKS, 2)),
                dma((CHUNKS, 2)),
                dma((tm_size, 2)),
                dma((2 * tm_size,)),
                dma((1,)),
            ],
            compiler_params=pltpu.CompilerParams(
                collective_id=0, has_side_effects=True, vmem_limit_bytes=60 * 2**20
            ),
        )(right_side, blocks, neighbors, shift_rates)
        block = pl.BlockSpec((2, steps, nodes), lambda e: (e, 0, 0))
        return pl.pallas_call(
            finish,
            grid=(plane // 2,),
            out_shape=jax.ShapeDtypeStruct(right_side.shape, f32),
            in_specs=[
                block,
                pl.BlockSpec((SWEEPS, half, nodes), lambda e: (0, 0, 0)),
                pl.BlockSpec((2, 2 * SWEEPS, nodes), lambda e: (e, 0, 0)),
            ],
            out_specs=block,
        )(series, table, start)

    return jax.shard_map(
        per_device,
        mesh=mesh,
        in_specs=(P("space", "tm", None), P("space", None, None, None), P("space", None), P()),
        out_specs=P("space", "tm", None),
        check_vma=False,
    )
```
